32 devices in a mesh: slab: 2 (over x), dp: 8 (over z, y), mp: 2 (over core).
Axes of the slice: x: 2, y: 2, z: 4, core: 2. Of those that a mesh axis runs over, the one named last changes fastest.
Arguments:
- states: bfloat16 [2, 8, 1024, 768], P('slab', 'dp', 'mp'), may hold values from -6 to 6
- attn_gain: bfloat16 [2, 768], P('slab', 'dp'), may hold values from 0.099609375 to 1.8984375
- w_query: bfloat16 [2, 768, 768], P('slab', 'dp', 'mp'), may hold values from -0.21875 to 0.21875
- w_key: bfloat16 [2, 768, 768], P('slab', 'dp', 'mp'), may hold values from -0.21875 to 0.21875
- w_value: bfloat16 [2, 768, 768], P('slab', 'dp', 'mp'), may hold values from -0.21875 to 0.21875
- w_out: bfloat16 [2, 768, 768], P('slab', 'mp', 'dp'), may hold values from -3.5 to 3.5
- mlp_gain: bfloat16 [2, 768], P('slab', 'dp'), may hold values from 0.099609375 to 1.8984375
- w_gate: bfloat16 [2, 768, 2048], P('slab', 'dp', 'mp'), may hold values from -0.21875 to 0.21875
- w_up: bfloat16 [2, 768, 2048], P('slab', 'dp', 'mp'), may hold values from -0.21875 to 0.21875
- w_down: bfloat16 [2, 2048, 768], P('slab', 'mp', 'dp'), may hold values from -0.125 to 0.125
- final_gain: bfloat16 [2, 768], P('slab', 'dp'), may hold values from 0.099609375 to 1.8984375
- cross_gain: bfloat16 [768], P(('slab', 'dp')), may hold values from 0.099609375 to 1.8984375
- cross_query: bfloat16 [768, 768], P(('slab', 'dp'), 'mp'), may hold values from -0.21875 to 0.21875
- cross_key: bfloat16 [768, 768], P(('slab', 'dp'), 'mp'), may hold values from -0.21875 to 0.21875
- cross_value: bfloat16 [768, 768], P(('slab', 'dp'), 'mp'), may hold values from -0.21875 to 0.21875
- cross_out: bfloat16 [768, 768], P('mp', ('slab', 'dp')), may hold values from -3.5 to 3.5
- embedding: bfloat16 [16384, 768], P(('slab', 'dp', 'mp')), may hold values from -8 to 8
- source_len: int32 [8], replicated, may hold values from 512 to 1024, as said below
- target_len: int32 [8], replicated, may hold values from 512 to 1024, as said below
- target_ids: int32 [8, 1024], P('dp'), may hold values from 0 to 16383
- pairing: int32 [8], replicated, may hold values from 0 to 7, each once
Outputs:
- seq_loss: float32 [8], P('dp')
- d_states: float32 [2, 8, 1024, 768], P('slab', 'dp', 'mp')
- g_attn_gain: float32 [2, 768], P('slab', 'dp')
- g_w_query: float32 [2, 768, 768], P('slab', 'dp', 'mp')
- g_w_key: float32 [2, 768, 768], P('slab', 'dp', 'mp')
- g_w_value: float32 [2, 768, 768], P('slab', 'dp', 'mp')
- g_w_out: float32 [2, 768, 768], P('slab', 'mp', 'dp')
- g_mlp_gain: float32 [2, 768], P('slab', 'dp')
- g_w_gate: float32 [2, 768, 2048], P('slab', 'dp', 'mp')
- g_w_up: float32 [2, 768, 2048], P('slab', 'dp', 'mp')
- g_w_down: float32 [2, 2048, 768], P('slab', 'mp', 'dp')
- g_final_gain: float32 [2, 768], P('slab', 'dp')
- g_cross_gain: float32 [768], P(('slab', 'dp'))
- g_cross_query: float32 [768, 768], P(('slab', 'dp'), 'mp')
- g_cross_key: float32 [768, 768], P(('slab', 'dp'), 'mp')
- g_cross_value: float32 [768, 768], P(('slab', 'dp'), 'mp')
- g_cross_out: float32 [768, 768], P('mp', ('slab', 'dp'))
- g_embedding: float32 [16384, 768], P(('slab', 'dp', 'mp'))
- token_loss: float32 [8, 1024], P('dp')
The draws below stay inside these ranges and needn't reach their ends.
Inputs may be any that keep to these rules, and one draw needn't show every extreme that they name: `source_len`: every source length lies between 512 and 1024, and some source sequence has exactly 1024 tokens. `target_len`: every target length lies between 512 and 1024, and some target sequence has exactly 1024 tokens. `pairing`: each source sequence is translated by exactly one target sequence.
All inputs are finite; a program needn't handle non-finite values.
Results may differ from the reference program's by a relative error of at most 0.025.
Values may be sent and summed in bfloat16 or wider, within the bound.
No kernel may reach another device: no remote copies, remote signals or barrier semaphores. Data moves between devices by JAX's collectives and lax.ppermute only.
A program may use at most 384 MiB of HBM per device.

```python
import math
import jax
import jax.numpy as jnp
import numpy as np
from jax import lax

D = 768
H = 12
DK = 64
FF = 2048
VOCAB = 16384
SLOT = 1024
SEQS = 8


def ragged_lengths(key, salt):
    salted = jax.random.fold_in(key, salt)
    first_key, second_key = jax.random.split(salted)
    lengths = jax.random.randint(first_key, (SEQS,), SLOT // 2, SLOT + 1)
    longest = jax.random.randint(second_key, (), 0, SEQS)
    return lengths.at[longest].set(SLOT).astype(jnp.int32)


def draw_source_len(key, part):
    return ragged_lengths(key, 11)


def draw_target_len(key, part):
    return ragged_lengths(key, 23)


def touch_ends(entries, key, smallest, top_value):
    longest = entries.shape.index(max(entries.shape))
    spots = []
    for shift in (0, 1):
        where = [jax.random.randint(jax.random.fold_in(key, axis), (), 0, length) for axis, length in enumerate(entries.shape)]
        where[longest] = (where[longest] + shift) % entries.shape[longest]
        spots.append(tuple(where))
    return entries.at[spots[0]].set(smallest).at[spots[1]].set(top_value)


def block_levels(rng, shape, cuts, smallest, top_value):
    def one(dim, shards_of):
        steps = jax.random.uniform(jax.random.fold_in(jax.random.fold_in(rng, 6), dim), (shards_of,), jnp.float32, smallest / len(cuts), top_value / len(cuts))
        return jnp.repeat(jnp.exp(steps), shape[dim] // shards_of).reshape((-1,) + (1,) * (len(shape) - dim - 1))

    factor_of = one(*cuts[0])
    for cut in cuts[1:]:
        factor_of = factor_of * one(*cut)
    return factor_of


def rank_bounds(number_of, lean):
    portions = [(1 << 20) // math.isqrt(standing ** lean) + 1 for standing in range(1, number_of + 1)]
    deviation = 1 + sum(portions) // (1 << 30)
    return np.cumsum(np.array([max(1, weight // deviation) for weight in portions]))


def ranked_ids(stream_key, shape, number_of, skew):
    listing = rank_bounds(number_of, skew)
    lot = jax.random.randint(jax.random.fold_in(stream_key, 1), shape, 0, int(listing[number_of - 1]))
    rank = jnp.searchsorted(jnp.asarray(listing, jnp.int32), lot, side="right")
    return jax.random.permutation(jax.random.fold_in(stream_key, 2), number_of)[rank].astype(jnp.int32)


def normal_values(rng, dims, scale, most, pieces=(), kind=jnp.bfloat16):
    drawn = scale * jax.random.normal(rng, dims, jnp.float32)
    if pieces:
        drawn = drawn * block_levels(rng, dims, pieces, -0.22, 0.18)
    return jnp.clip(drawn, -most, most).astype(kind)


def setup_inputs(seed: int = 0) -> dict:
    key_of = jax.random.split(jax.random.key(seed), 22)
    states = normal_values(key_of[0], (2, SEQS, SLOT, D), 1.0, 6.0, ((0, 2), (1, 8), (2, 2)))
    attn_gain = jnp.clip(1.0 + 0.18 * jax.random.normal(key_of[1], (2, D), jnp.float32), 0.099609375, 1.8984375).astype(jnp.bfloat16)
    w_query = normal_values(key_of[2], (2, D, H * DK), D ** -0.5, 0.21875, ((0, 2), (1, 8), (2, 2)))
    w_key = normal_values(key_of[3], (2, D, H * DK), D ** -0.5, 0.21875, ((0, 2), (1, 8), (2, 2)))
    w_value = normal_values(key_of[4], (2, D, H * DK), D ** -0.5, 0.21875, ((0, 2), (1, 8), (2, 2)))
    w_out = normal_values(key_of[5], (2, H * DK, D), 3 ** -0.5, 3.5, ((0, 2), (1, 2), (2, 8)))
    mlp_gain = jnp.clip(1.0 + 0.18 * jax.random.normal(key_of[6], (2, D), jnp.float32), 0.099609375, 1.8984375).astype(jnp.bfloat16)
    w_gate = normal_values(key_of[7], (2, D, FF), D ** -0.5, 0.21875, ((0, 2), (1, 8), (2, 2)))
    w_up = normal_values(key_of[8], (2, D, FF), D ** -0.5, 0.21875, ((0, 2), (1, 8), (2, 2)))
    w_down = normal_values(key_of[9], (2, FF, D), FF ** -0.5, 0.125, ((0, 2), (1, 2), (2, 8)))
    final_gain = jnp.clip(1.0 + 0.18 * jax.random.normal(key_of[10], (2, D), jnp.float32), 0.099609375, 1.8984375).astype(jnp.bfloat16)
    cross_gain = jnp.clip(1.0 + 0.18 * jax.random.normal(key_of[11], (D,), jnp.float32), 0.099609375, 1.8984375).astype(jnp.bfloat16)
    cross_query = normal_values(key_of[12], (D, H * DK), D ** -0.5, 0.21875, ((0, 16), (1, 2)))
    cross_key = normal_values(key_of[13], (D, H * DK), D ** -0.5, 0.21875, ((0, 16), (1, 2)))
    cross_value = normal_values(key_of[14], (D, H * DK), D ** -0.5, 0.21875, ((0, 16), (1, 2)))
    cross_out = normal_values(key_of[15], (H * DK, D), 3 ** -0.5, 3.5, ((0, 2), (1, 16)))
    embedding = normal_values(key_of[16], (VOCAB, D), 2.0, 8.0, ((0, 32),))
    source_len = draw_source_len(jax.random.fold_in(key_of[21], 71), 0)
    target_len = draw_target_len(jax.random.fold_in(key_of[21], 71), 0)
    target_ids = touch_ends(ranked_ids(key_of[19], (SEQS, SLOT), VOCAB, 1), jax.random.fold_in(key_of[19], 3), 0, VOCAB - 1).astype(jnp.int32)
    pairing = jax.random.permutation(key_of[20], SEQS).astype(jnp.int32)
    return dict(states=states, attn_gain=attn_gain, w_query=w_query, w_key=w_key, w_value=w_value, w_out=w_out, mlp_gain=mlp_gain, w_gate=w_gate, w_up=w_up, w_down=w_down, final_gain=final_gain, cross_gain=cross_gain, cross_query=cross_query, cross_key=cross_key, cross_value=cross_value, cross_out=cross_out, embedding=embedding, source_len=source_len, target_len=target_len, target_ids=target_ids, pairing=pairing)


@jax.custom_vjp
def low(v):
    return lax.optimization_barrier(v.astype(jnp.bfloat16)).astype(jnp.float32)

@jax.custom_vjp
def low_back(v):
    return v

def low_keep(v):
    return (low(v), None)

def low_pass(kept, grad):
    return (grad,)

def back_keep(v):
    return (v, None)

def back_low(kept, grad):
    return (low(grad),)
low.defvjp(low_keep, low_pass)
low_back.defvjp(back_keep, back_low)
highest = lax.Precision.HIGHEST
epsilon = 1e-06
masked_out = -1000000000.0

def rounded(operand):
    return low(low_back(operand))

def matmul(matrix_a, matrix_b):
    return jnp.dot(matrix_a, matrix_b, precision=highest)

def rms_apply(hidden, scaling):
    return hidden * lax.rsqrt(lax.optimization_barrier(jnp.mean(hidden * hidden, axis=-1, keepdims=True)) + epsilon) * scaling

def attention(query_in, memory_in, w_query, w_key, w_value, w_out, allowed):
    query_rows = query_in.shape[0]
    memory_rows = memory_in.shape[0]
    queries = rounded(matmul(query_in, w_query)).reshape(query_rows, H, DK)
    key_rows = rounded(matmul(memory_in, w_key)).reshape(memory_rows, H, DK)
    value_rows = rounded(matmul(memory_in, w_value)).reshape(memory_rows, H, DK)
    scores = low_back(jnp.einsum('qhd,khd->hqk', queries, key_rows, precision=highest) * DK ** (-0.5))
    scores = jnp.where(allowed[None], scores, masked_out)
    shifted = jnp.exp(scores - lax.optimization_barrier(jnp.max(scores, axis=-1, keepdims=True)))
    weights = low(shifted / lax.optimization_barrier(jnp.sum(shifted, axis=-1, keepdims=True)))
    context = jnp.einsum('hqk,khd->qhd', weights, value_rows, precision=highest)
    context = rounded(context.reshape(query_rows, H * DK))
    return low_back(matmul(context, w_out))

def feed_forward(hidden_in, gain_mlp, w_gate, w_up, w_down):
    normed = low(rms_apply(hidden_in, gain_mlp))
    gate_out = low_back(matmul(normed, w_gate))
    up_out = low_back(matmul(normed, w_up))
    inner = low(jax.nn.gelu(gate_out, approximate=True) * up_out)
    return hidden_in + low_back(matmul(inner, w_down))

def encode(layer, hidden_in, source_length):
    gain_attn, w_query, w_key, w_value, w_out, gain_mlp, w_gate, w_up, w_down, gain_final = layer
    positions = jnp.arange(SLOT)
    allowed = jnp.broadcast_to(positions[None, :] < source_length, (SLOT, SLOT))
    normed = low(rms_apply(hidden_in, gain_attn))
    hidden = hidden_in + attention(normed, normed, w_query, w_key, w_value, w_out, allowed)
    hidden = feed_forward(hidden, gain_mlp, w_gate, w_up, w_down)
    return rounded(rms_apply(hidden, gain_final))

def decode(layer, cross, vocab_table, hidden_in, memory, target_length, source_length, wanted_ids):
    gain_attn, w_query, w_key, w_value, w_out, gain_mlp, w_gate, w_up, w_down, gain_final = layer
    gain_cross, query_cross, key_cross, value_cross, out_cross = cross
    positions = jnp.arange(SLOT)
    self_allowed = (positions[None, :] <= positions[:, None]) & (positions[None, :] < target_length)
    cross_allowed = jnp.broadcast_to(positions[None, :] < source_length, (SLOT, SLOT))
    normed = low(rms_apply(hidden_in, gain_attn))
    hidden = hidden_in + attention(normed, normed, w_query, w_key, w_value, w_out, self_allowed)
    normed_cross = low(rms_apply(hidden, gain_cross))
    hidden = hidden + attention(normed_cross, memory, query_cross, key_cross, value_cross, out_cross, cross_allowed)
    hidden = feed_forward(hidden, gain_mlp, w_gate, w_up, w_down)
    final_rows = low(rms_apply(hidden, gain_final))
    logits = low_back(matmul(final_rows, vocab_table.T) * D ** (-0.5))
    log_total = jax.nn.logsumexp(logits, axis=-1)
    picked = jnp.take_along_axis(logits, wanted_ids[:, None], axis=1)[:, 0]
    return jnp.where(positions < target_length, log_total - picked, 0.0)

def reference(states, attn_gain, w_query, w_key, w_value, w_out, mlp_gain, w_gate, w_up, w_down, final_gain, cross_gain, cross_query, cross_key, cross_value, cross_out, embedding, source_len, target_len, target_ids, pairing):
    floats = tuple((operand.astype(jnp.float32) for operand in (states, attn_gain, w_query, w_key, w_value, w_out, mlp_gain, w_gate, w_up, w_down, final_gain, cross_gain, cross_query, cross_key, cross_value, cross_out, embedding)))

    def objective(params):
        encoder_layer = tuple((stacked[0] for stacked in params[1:11]))
        decoder_layer = tuple((stacked[1] for stacked in params[1:11]))
        cross_layer = params[11:16]
        vocab_table = params[16]

        def encode_one(packed):
            return encode(encoder_layer, packed[0], packed[1])
        memories = lax.map(jax.checkpoint(encode_one), (params[0][0], source_len))

        def decode_one(packed):
            return decode(decoder_layer, cross_layer, vocab_table, packed[0], packed[1], packed[2], packed[3], packed[4])
        per_token = lax.map(jax.checkpoint(decode_one), (params[0][1], memories[pairing], target_len, source_len[pairing], target_ids))
        return (jnp.sum(per_token), per_token)
    total_ce, pullback, per_token = jax.vjp(objective, floats, has_aux=True)
    gradients, = pullback(jnp.ones_like(total_ce))
    seq_loss = lax.optimization_barrier(jnp.sum(per_token, axis=1)) / target_len.astype(per_token.dtype)
    return (seq_loss, gradients[0], gradients[1], gradients[2], gradients[3], gradients[4], gradients[5], gradients[6], gradients[7], gradients[8], gradients[9], gradients[10], gradients[11], gradients[12], gradients[13], gradients[14], gradients[15], gradients[16], per_token)
```

```python
import jax
import jax.numpy as jnp
from jax import lax
from jax.experimental import pallas as pl
from jax.experimental.pallas import tpu as pltpu
from jax.sharding import PartitionSpec as P

DK = 64
f32 = jnp.float32
bf16 = jnp.bfloat16
epsilon = 1e-06
masked_out = -1000000000.0


def loop_order(count):
    return [0, 2, 4, 6, 7, 5, 3, 1] if count == 8 else None


def swap_core(value):
    return lax.ppermute(value, "mp", [(0, 1), (1, 0)])


def swap_slab(value):
    return lax.ppermute(value, "slab", [(0, 1), (1, 0)])


def to_encoder(value):
    return lax.ppermute(value, "slab", [(1, 0)])


def to_decoder(value):
    return lax.ppermute(value, "slab", [(0, 1)])


def loop_step(value, order, step):
    count = len(order)
    return lax.ppermute(
        value, "dp", [(order[i], order[(i + step) % count]) for i in range(count)]
    )


def held_after(value, earlier):
    return value if earlier is None else lax.optimization_barrier((value, earlier))[0]


def loop_index(offset):
    order = loop_order(lax.axis_size("dp"))
    place_of = jnp.array([order.index(i) for i in range(len(order))], jnp.int32)
    place = place_of[lax.axis_index("dp")]
    return jnp.array(order, jnp.int32)[(place + offset) % len(order)]


def loop_gather(block):
    order = loop_order(lax.axis_size("dp"))
    half = block.shape[0] // 2
    behind, ahead = [block], [block]
    for _ in range(3):
        behind.append(loop_step(behind[-1], order, 1))
        ahead.append(loop_step(ahead[-1], order, -1))
    far = jnp.concatenate(
        [loop_step(behind[3][:half], order, 1), loop_step(ahead[3][half:], order, -1)], 0
    )
    offsets = [0, -1, 1, -2, 2, -3, 3, 4]
    blocks = [block, behind[1], ahead[1], behind[2], ahead[2], behind[3], ahead[3], far]
    return offsets, blocks


def loop_scatter(chunk, rows):
    order = loop_order(lax.axis_size("dp"))
    half = rows // 2
    first = chunk(4)
    right = loop_step(first[:half].astype(bf16), order, 1)
    left = loop_step(first[half:].astype(bf16), order, -1)
    mine = chunk(3)
    right = jnp.concatenate([(mine[:half] + right).astype(bf16), mine[half:].astype(bf16)], 0)
    right = loop_step(right, order, 1)
    mine = chunk(-3)
    left = jnp.concatenate([mine[:half].astype(bf16), (mine[half:] + left).astype(bf16)], 0)
    left = loop_step(left, order, -1)
    for offset in (2, 1):
        right = loop_step((chunk(offset) + right).astype(bf16), order, 1)
        left = loop_step((chunk(-offset) + left).astype(bf16), order, -1)
    return chunk(0) + right.astype(f32) + left.astype(f32)


def assemble(blocks, indices, widths):
    count, (rows, _) = len(blocks), blocks[0].shape

    def body(index_ref, *refs):
        sources, targets = refs[:count], refs[count:]
        for turn in range(count):

            @pl.when(pl.program_id(0) == turn)
            def _():
                first = 0
                for target, width in zip(targets, widths):
                    target[0] = sources[turn][:, first : first + width]
                    first += width

    whole = [pl.BlockSpec(block.shape, lambda i, index: (0, 0)) for block in blocks]
    parts = [pl.BlockSpec((1, rows, width), lambda i, index: (index[i], 0, 0)) for width in widths]
    size = sum(block.size for block in blocks) * 4
    out = pl.pallas_call(
        body,
        out_shape=[jax.ShapeDtypeStruct((count, rows, w), blocks[0].dtype) for w in widths],
        grid_spec=pltpu.PrefetchScalarGridSpec(
            num_scalar_prefetch=1, grid=(count,), in_specs=whole, out_specs=parts
        ),
        cost_estimate=pl.CostEstimate(flops=0, bytes_accessed=size, transcendentals=0),
        name="assemble",
    )(jnp.stack(indices), *blocks)
    return [part.reshape(count * rows, part.shape[2]) for part in out]


def gather_columns(block, widths, earlier=None):
    block = held_after(block, earlier)
    if loop_order(lax.axis_size("dp")) is None:
        rows = lax.all_gather(block, "dp", axis=0, tiled=True)
        cuts = [sum(widths[:i]) for i in range(1, len(widths))]
        return jnp.split(rows, cuts, axis=1), None
    offsets, blocks = loop_gather(block)
    parts = assemble(blocks, [loop_index(offset) for offset in offsets], widths)
    return parts, blocks[-1]


def gather_table(block, first_id, step_id, earlier=None):
    block = held_after(block, earlier)
    rows = block.shape[0]
    line = jnp.arange(rows, dtype=jnp.int32)
    if loop_order(lax.axis_size("dp")) is None:
        table = lax.all_gather(block, "dp", axis=0, tiled=True)
        starts = first_id + step_id * jnp.arange(lax.axis_size("dp"), dtype=jnp.int32)
        return [table], [(starts[:, None] + line[None, :]).reshape(-1)]
    offsets, blocks = loop_gather(block)
    return blocks, [first_id + step_id * loop_index(offset) + line for offset in offsets]


def scatter_rows(parts):
    count = lax.axis_size("dp")
    rows, columns = parts[0].shape[0] // count, parts[0].shape[1]
    if loop_order(count) is None:
        total = sum(part.astype(f32) for part in parts).astype(bf16)
        return lax.psum_scatter(total, "dp", scatter_dimension=0, tiled=True).astype(f32)
    stacks = [part.reshape(count, rows, columns) for part in parts]

    def chunk(offset):
        where = loop_index(offset)
        return sum(
            lax.dynamic_index_in_dim(stack, where, 0, keepdims=False).astype(f32) for stack in stacks
        )

    return loop_scatter(chunk, rows)


def scatter_table(pieces):
    if loop_order(lax.axis_size("dp")) is None:
        return lax.psum_scatter(
            pieces[0].astype(bf16), "dp", scatter_dimension=0, tiled=True
        ).astype(f32)
    offsets = [0, -1, 1, -2, 2, -3, 3, 4]
    return loop_scatter(lambda offset: pieces[offsets.index(offset)].astype(f32), pieces[0].shape[0])


def to_distance(value, distance):
    count = lax.axis_size("dp")
    return lax.ppermute(value, "dp", [(i, (i + distance) % count) for i in range(count)])


def gather_small(value):
    count = lax.axis_size("dp")
    if loop_order(count) is None:
        return lax.all_gather(value, "dp")
    me = lax.axis_index("dp")
    received = [to_distance(value, distance) for distance in range(count - 1, 0, -1)] + [value]
    twice = jnp.stack(received + received)
    return lax.dynamic_slice_in_dim(twice, (count - 1 - me) % count, count, 0)


def scatter_small(pieces):
    count = lax.axis_size("dp")
    if loop_order(count) is None:
        return lax.psum_scatter(pieces, "dp", scatter_dimension=0)
    me = lax.axis_index("dp")
    total = lax.dynamic_index_in_dim(pieces, me, 0, keepdims=False)
    for distance in range(1, count):
        piece = lax.dynamic_index_in_dim(pieces, (me + distance) % count, 0, keepdims=False)
        total = total + to_distance(piece, distance)
    return total


def reroute_plane(rows, source_of):
    count = lax.axis_size("dp")
    pieces = rows.reshape(count, rows.shape[0] // count, rows.shape[1])
    if loop_order(count) is None:
        spread = lax.all_to_all(pieces, "dp", split_axis=0, concat_axis=0, tiled=True)
        back = lax.all_to_all(spread[source_of], "dp", split_axis=0, concat_axis=0, tiled=True)
        return back.reshape(rows.shape)
    me = lax.axis_index("dp")

    def piece_at(stack, where):
        return lax.dynamic_index_in_dim(stack, where, 0, keepdims=False)

    received = [piece_at(pieces, me)]
    for distance in range(1, count):
        received.append(to_distance(piece_at(pieces, (me + distance) % count), distance))
    held = jnp.stack(received)
    final = [piece_at(held, (me - source_of[me]) % count)]
    for distance in range(1, count):
        goal = (me + distance) % count
        final.append(to_distance(piece_at(held, (me - source_of[goal]) % count), distance))
    return assemble(final, [(me - distance) % count for distance in range(count)], [rows.shape[1]])[0]


def reroute_decoder(rows, source_of, decoding):
    half = rows.shape[0] // 2
    lent = jnp.where(decoding, rows[half:], to_encoder(rows[:half]))
    moved = reroute_plane(lent, source_of)
    return jnp.concatenate([to_decoder(moved), moved], 0)


def matmul(a, b):
    return jnp.dot(a, b, preferred_element_type=f32)


def contract_last(a, b):
    return lax.dot_general(a, b, (((1,), (1,)), ((), ())), preferred_element_type=f32)


def contract_first(a, b):
    return lax.dot_general(a, b, (((0,), (0,)), ((), ())), preferred_element_type=f32)


def rms_apply(hidden, gain):
    return hidden * lax.rsqrt(jnp.mean(hidden * hidden, axis=-1, keepdims=True) + epsilon) * gain


def norm_back(hidden, gain, upstream):
    scale = lax.rsqrt(jnp.mean(hidden * hidden, axis=-1, keepdims=True) + epsilon)
    weighted = upstream * gain
    dot = jnp.mean(weighted * hidden, axis=-1, keepdims=True)
    grad = scale * weighted - hidden * (scale * scale * scale * dot)
    return grad, jnp.sum(upstream * hidden * scale, axis=0)


def side(a, pair):
    return jnp.concatenate([matmul(a, pair[0]), matmul(a, pair[1])], 1)


def heads(rows):
    return rows.reshape(rows.shape[0], -1, DK)


def attend(queries, key_rows, value_rows, allowed):
    scores = jnp.einsum("qhd,khd->hqk", heads(queries), heads(key_rows), preferred_element_type=f32)
    scores = jnp.where(allowed[None], scores * DK ** (-0.5), masked_out)
    highest = jnp.max(scores, axis=-1, keepdims=True)
    shifted = jnp.exp(scores - highest)
    totals = jnp.sum(shifted, axis=-1, keepdims=True)
    weights = (shifted / totals).astype(bf16)
    context = jnp.einsum("hqk,khd->qhd", weights, heads(value_rows), preferred_element_type=f32)
    return context.reshape(queries.shape).astype(bf16), highest + jnp.log(totals)


def attend_back(queries, key_rows, value_rows, allowed, log_total, grad_context):
    scale = DK ** (-0.5)
    queries, key_rows, value_rows = heads(queries), heads(key_rows), heads(value_rows)
    grad_heads = heads(grad_context)
    scores = jnp.einsum("qhd,khd->hqk", queries, key_rows, preferred_element_type=f32) * scale
    scores = jnp.where(allowed[None], scores, masked_out)
    weights = jnp.exp(scores - log_total)
    grad_weights = jnp.einsum("qhd,khd->hqk", grad_heads, value_rows, preferred_element_type=f32)
    grad_scores = weights * (grad_weights - jnp.sum(grad_weights * weights, axis=-1, keepdims=True))
    grad_scores = grad_scores.astype(bf16)

    def flat(grad):
        return grad.reshape(grad.shape[0], -1).astype(bf16)

    grad_query = jnp.einsum("hqk,khd->qhd", grad_scores, key_rows, preferred_element_type=f32)
    grad_key = jnp.einsum("hqk,qhd->khd", grad_scores, queries, preferred_element_type=f32)
    grad_value = jnp.einsum(
        "hqk,qhd->khd", weights.astype(bf16), grad_heads, preferred_element_type=f32
    )
    return flat(grad_query * scale), flat(grad_key * scale), flat(grad_value)


def attention_forward(query_in, memory_in, qkv, out, allowed):
    width = qkv[0].shape[1] // 3
    queries = side(query_in, [part[:, :width] for part in qkv]).astype(bf16)
    key_rows = side(memory_in, [part[:, width : 2 * width] for part in qkv]).astype(bf16)
    value_rows = side(memory_in, [part[:, 2 * width :] for part in qkv]).astype(bf16)
    context, log_total = attend(queries, key_rows, value_rows, allowed)
    branch = contract_last(context[:, :width], out[0]) + contract_last(context[:, width:], out[1])
    return branch, (queries, key_rows, value_rows, context, log_total)


def attention_back(kept, qkv, out, allowed, grad_rows):
    queries, key_rows, value_rows, context, log_total = kept
    width = qkv[0].shape[1] // 3
    grad_context = side(grad_rows, out).astype(bf16)
    grads = attend_back(queries, key_rows, value_rows, allowed, log_total, grad_context)

    def into(grad, start):
        return sum(
            contract_last(grad[:, i * width : (i + 1) * width], qkv[i][:, start : start + width])
            for i in range(2)
        )

    grad_query_in = into(grads[0], 0)
    grad_memory = into(grads[1], width) + into(grads[2], 2 * width)
    return grads, grad_query_in, grad_memory


def attention_weight_grads(query_in, memory_in, context, grads, grad_rows):
    width = context.shape[1] // 2
    parts = []
    for i in range(2):
        cut = slice(i * width, (i + 1) * width)
        parts.append(
            jnp.concatenate(
                [
                    contract_first(query_in, grads[0][:, cut]).astype(bf16),
                    contract_first(memory_in, grads[1][:, cut]).astype(bf16),
                    contract_first(memory_in, grads[2][:, cut]).astype(bf16),
                    contract_first(grad_rows, context[:, cut]).astype(bf16),
                ],
                1,
            )
        )
    return parts


def mlp_forward(normed, gate_up, down):
    width = down[0].shape[1]
    both = [matmul(normed, part) for part in gate_up]
    gate_out = [part[:, :width] for part in both]
    up_out = [part[:, width:] for part in both]
    inner = [
        (jax.nn.gelu(gate, approximate=True) * up).astype(bf16) for gate, up in zip(gate_out, up_out)
    ]
    branch = contract_last(inner[0], down[0]) + contract_last(inner[1], down[1])
    return branch, (both, inner)


def gelu_gate(gate_out, up_out):
    return jax.nn.gelu(gate_out, approximate=True) * up_out


def mlp_back(kept, gate_up, down, grad_rows):
    both, _ = kept
    width = down[0].shape[1]
    grads, total = [], 0.0
    for i in range(2):
        grad_inner = matmul(grad_rows, down[i])
        _, pullback = jax.vjp(gelu_gate, both[i][:, :width], both[i][:, width:])
        grad = jnp.concatenate([part.astype(bf16) for part in pullback(grad_inner)], 1)
        grads.append(grad)
        total = total + contract_last(grad, gate_up[i])
    return grads, total


def mlp_weight_grads(normed, inner, grads, grad_rows):
    return [
        jnp.concatenate(
            [
                contract_first(normed, grads[i]).astype(bf16),
                contract_first(grad_rows, inner[i]).astype(bf16),
            ],
            1,
        )
        for i in range(2)
    ]


def merge_stats(first, second):
    highest = jnp.maximum(first[0], second[0])
    totals = first[1] * jnp.exp(first[0] - highest) + second[1] * jnp.exp(second[0] - highest)
    return jnp.stack([highest, totals, first[2] + second[2]])


def on_device(
    states,
    attn_gain,
    w_query,
    w_key,
    w_value,
    w_out,
    mlp_gain,
    w_gate,
    w_up,
    w_down,
    final_gain,
    cross_gain,
    cross_query,
    cross_key,
    cross_value,
    cross_out,
    embedding,
    source_len,
    target_len,
    target_ids,
    pairing,
):
    slab, me, core = (lax.axis_index(name) for name in ("slab", "dp", "mp"))
    decoding = slab == 1
    count = lax.axis_size("dp")
    numbers = jnp.arange(count, dtype=jnp.int32)
    target_of = jnp.sum(
        jnp.where(pairing[None, :] == numbers[:, None], numbers[None, :], 0), axis=1
    )
    target = target_of[me]
    source_length, target_length = source_len[me], target_len[target]

    gain_rows = attn_gain.shape[1]
    cross_rows = cross_gain.shape[0]
    gains = gather_small(
        jnp.concatenate([attn_gain[0], mlp_gain[0], final_gain[0], cross_gain], 0)
    ).astype(f32)
    gain_attn, gain_mlp, gain_final = (
        gains[:, i * gain_rows : (i + 1) * gain_rows].reshape(-1) for i in range(3)
    )
    cross_part = gains[:, 3 * gain_rows :].reshape(-1)
    gain_cross = jnp.concatenate([to_decoder(cross_part), cross_part], 0)
    wanted = lax.dynamic_index_in_dim(gather_small(target_ids[0]), target, 0, keepdims=False)

    rows = states[0, 0]
    own = jnp.where(decoding, reroute_decoder(rows, target_of, decoding), rows)
    other = swap_core(own)

    width, hidden = w_query.shape[2], w_gate.shape[2]
    (qkv, out), last = gather_columns(
        jnp.concatenate([w_query[0], w_key[0], w_value[0], w_out[0].T], 1), [3 * width, width]
    )
    qkv, out = (qkv, swap_core(qkv)), (out, swap_core(out))
    (gate_up, down), last = gather_columns(
        jnp.concatenate([w_gate[0], w_up[0], w_down[0].T], 1), [2 * hidden, hidden], last
    )
    gate_up, down = (gate_up, swap_core(gate_up)), (down, swap_core(down))
    (cross_qkv, cross_o), last = gather_columns(
        jnp.concatenate([cross_query, cross_key, cross_value, cross_out.T], 1),
        [3 * width, width],
        last,
    )
    cross_qkv = jnp.concatenate([to_decoder(cross_qkv), cross_qkv], 0)
    cross_o = jnp.concatenate([to_decoder(cross_o), cross_o], 0)
    cross_qkv, cross_o = (cross_qkv, swap_core(cross_qkv)), (cross_o, swap_core(cross_o))
    vocab_rows = embedding.shape[0]
    cores = lax.axis_size("mp")
    tables, entries = gather_table(
        embedding,
        (slab * count * cores + core) * vocab_rows,
        cores * vocab_rows,
        last,
    )

    half = rows.shape[0]
    line = jnp.arange(half, dtype=jnp.int32)
    query_at = core * half + line
    key_at = jnp.concatenate([query_at, (1 - core) * half + line])
    own_length = jnp.where(decoding, target_length, source_length)
    later = key_at[None, :] > query_at[:, None]
    self_allowed = (key_at[None, :] < own_length) & jnp.logical_not(later & decoding)
    cross_allowed = jnp.broadcast_to(key_at[None, :] < source_length, (half, 2 * half))

    start = own.astype(f32)
    normed = rms_apply(start, gain_attn).astype(bf16)
    normed_all = jnp.concatenate([normed, rms_apply(other.astype(f32), gain_attn).astype(bf16)], 0)
    branch, self_kept = attention_forward(normed, normed_all, qkv, out, self_allowed)
    after_self = start + branch

    normed_enc = rms_apply(after_self, gain_mlp).astype(bf16)
    branch, enc_kept = mlp_forward(normed_enc, gate_up, down)
    after_enc = after_self + branch
    memory = to_decoder(rms_apply(after_enc, gain_final).astype(bf16))
    memory = jnp.concatenate([memory, swap_core(memory)], 0)

    normed_cross = rms_apply(after_self, gain_cross).astype(bf16)
    branch, cross_kept = attention_forward(normed_cross, memory, cross_qkv, cross_o, cross_allowed)
    after_cross = after_self + branch
    normed_dec = rms_apply(after_cross, gain_mlp).astype(bf16)
    branch, dec_kept = mlp_forward(normed_dec, gate_up, down)
    after_mlp = after_cross + branch
    final = rms_apply(after_mlp, gain_final).astype(bf16)

    final = jnp.where(decoding, final, to_encoder(final))
    final = jnp.concatenate([final, swap_core(final)], 0)
    wanted = jnp.where(core == 0, wanted, jnp.roll(wanted, half))
    counted = key_at < target_length
    width_scale = final.shape[1] ** (-0.5)
    logits = [contract_last(final, table) * width_scale for table in tables]
    hits = [ids[None, :] == wanted[:, None] for ids in entries]
    highest = jnp.max(jnp.stack([jnp.max(part, axis=1) for part in logits]), axis=0)
    totals = sum(jnp.sum(jnp.exp(part - highest[:, None]), axis=1) for part in logits)
    picked = sum(jnp.sum(jnp.where(hit, part, 0.0), axis=1) for hit, part in zip(hits, logits))
    stats = jnp.stack([highest, totals, picked])
    flipped = jnp.roll(swap_core(stats), half, axis=1)
    stats = merge_stats(stats, flipped)
    stats = merge_stats(stats, swap_slab(stats))
    log_total = stats[0] + jnp.log(stats[1])
    token_ce = jnp.where(counted, log_total - stats[2], 0.0)
    in_order = jnp.where(core == 0, token_ce, jnp.roll(token_ce, half))
    token_loss = lax.dynamic_index_in_dim(gather_small(in_order), pairing[me], 0, keepdims=True)
    seq_loss = jnp.sum(token_loss, axis=1) / target_len[me].astype(f32)

    grad_logits = [
        jnp.where(
            counted[:, None], jnp.exp(part - log_total[:, None]) - hit.astype(f32), 0.0
        ).astype(bf16)
        for hit, part in zip(hits, logits)
    ]
    grad_final = sum(matmul(part, table) for part, table in zip(grad_logits, tables)) * width_scale
    grad_final = grad_final[:half] + swap_core(grad_final[half:].astype(bf16)).astype(f32)
    grad_final = grad_final + to_decoder(grad_final.astype(bf16)).astype(f32)
    grad_final = jnp.where(decoding, grad_final, 0.0)
    grad_table = [contract_first(part, final) * width_scale for part in grad_logits]
    g_embedding = scatter_table(grad_table)

    stream, grad_gain_final = norm_back(after_mlp, gain_final, grad_final)
    dec_rows = stream.astype(bf16)
    dec_grads, grad_normed = mlp_back(dec_kept, gate_up, down, dec_rows)
    part, grad_gain_mlp = norm_back(after_cross, gain_mlp, grad_normed)
    stream = stream + part
    cross_in = stream.astype(bf16)
    cross_grads, grad_normed, grad_memory = attention_back(
        cross_kept, cross_qkv, cross_o, cross_allowed, cross_in
    )
    grad_memory = grad_memory[:half] + swap_core(grad_memory[half:].astype(bf16)).astype(f32)
    grad_memory = to_encoder(grad_memory.astype(bf16)).astype(f32)
    part, grad_gain_cross = norm_back(after_self, gain_cross, grad_normed)
    stream = stream + part
    cross_weights = attention_weight_grads(
        normed_cross, memory, cross_kept[3], cross_grads, cross_in
    )

    enc_stream, gain_part = norm_back(after_enc, gain_final, grad_memory)
    grad_gain_final = grad_gain_final + gain_part
    enc_rows = enc_stream.astype(bf16)
    enc_grads, grad_normed = mlp_back(enc_kept, gate_up, down, enc_rows)
    part, gain_part = norm_back(after_self, gain_mlp, grad_normed)
    grad_gain_mlp = grad_gain_mlp + gain_part
    stream = stream + enc_stream + part
    mlp_weights = lax.cond(
        decoding,
        lambda dec, enc: mlp_weight_grads(*dec),
        lambda dec, enc: mlp_weight_grads(*enc),
        (normed_dec, dec_kept[1], dec_grads, dec_rows),
        (normed_enc, enc_kept[1], enc_grads, enc_rows),
    )

    self_in = stream.astype(bf16)
    self_grads, grad_normed, grad_keyside = attention_back(
        self_kept, qkv, out, self_allowed, self_in
    )
    grad_normed = grad_normed + grad_keyside[:half]
    grad_normed = grad_normed + swap_core(grad_keyside[half:].astype(bf16)).astype(f32)
    part, grad_gain_attn = norm_back(start, gain_attn, grad_normed)
    stream = stream + part
    self_weights = attention_weight_grads(normed, normed_all, self_kept[3], self_grads, self_in)
    d_states = jnp.where(
        decoding, reroute_decoder(stream.astype(bf16), pairing, decoding).astype(f32), stream
    )

    def owned(parts):
        return scatter_rows([parts[0], swap_core(parts[1])])

    def plane_half(value):
        top, bottom = value[: value.shape[0] // 2], value[value.shape[0] // 2 :]
        return jnp.where(decoding, bottom, to_encoder(top))

    g_cross = owned([plane_half(part) for part in cross_weights])
    g_mlp = owned(mlp_weights)
    g_attn = owned(self_weights)

    gain_grads = jnp.stack([grad_gain_attn, grad_gain_mlp, grad_gain_final, grad_gain_cross])
    gain_grads = gain_grads + swap_core(gain_grads)
    packed = jnp.concatenate(
        [gain_grads[i].reshape(count, gain_rows) for i in range(3)]
        + [plane_half(gain_grads[3]).reshape(count, cross_rows)],
        1,
    )
    gain_own = scatter_small(packed)[None]

    return (
        seq_loss,
        d_states[None, None],
        gain_own[:, :gain_rows],
        g_attn[None, :, :width],
        g_attn[None, :, width : 2 * width],
        g_attn[None, :, 2 * width : 3 * width],
        g_attn[:, 3 * width :].T[None],
        gain_own[:, gain_rows : 2 * gain_rows],
        g_mlp[None, :, :hidden],
        g_mlp[None, :, hidden : 2 * hidden],
        g_mlp[:, 2 * hidden :].T[None],
        gain_own[:, 2 * gain_rows : 3 * gain_rows],
        gain_own[0, 3 * gain_rows :],
        g_cross[:, :width],
        g_cross[:, width : 2 * width],
        g_cross[:, 2 * width : 3 * width],
        g_cross[:, 3 * width :].T,
        g_embedding,
        token_loss,
    )


def solution(mesh):
    layer = P("slab", "dp", "mp")
    shared = P(("slab", "dp"), "mp")
    gain = P("slab", "dp")
    turned = P("slab", "mp", "dp")
    tokens = P("slab", "dp", "mp", None)
    weights = (gain, layer, layer, layer, turned, gain, layer, layer, turned, gain)
    crossing = (P(("slab", "dp")), shared, shared, shared, P("mp", ("slab", "dp")))
    table = P(("slab", "dp", "mp"), None)
    return jax.shard_map(
        on_device,
        mesh=mesh,
        in_specs=(tokens,) + weights + crossing + (table, P(), P(), P("dp", None), P()),
        out_specs=(P("dp"), tokens) + weights + crossing + (table, P("dp", None)),
        check_vma=False,
    )
```

```python
import jax
import jax.numpy as jnp
from jax import lax
from jax.experimental import pallas as pl
from jax.experimental.pallas import tpu as pltpu
from jax.sharding import PartitionSpec as P

DK = 64
f32 = jnp.float32
bf16 = jnp.bfloat16
epsilon = 1e-06
masked_out = -1000000000.0


def loop_order(count):
    return [0, 2, 4, 6, 7, 5, 3, 1] if count == 8 else None


def swap_core(value):
    return lax.ppermute(value, "mp", [(0, 1), (1, 0)])


def swap_slab(value):
    return lax.ppermute(value, "slab", [(0, 1), (1, 0)])


def to_encoder(value):
    return lax.ppermute(value, "slab", [(1, 0)])


def to_decoder(value):
    return lax.ppermute(value, "slab", [(0, 1)])


def loop_step(value, step):
    order = loop_order(lax.axis_size("dp"))
    count = len(order)
    pairs = [(order[i], order[(i + step) % count]) for i in range(count)]
    return lax.ppermute(value, "dp", pairs)


def held_after(value, earlier):
    return value if earlier is None else lax.optimization_barrier((value, earlier))[0]


def loop_index(offset):
    me, count = lax.axis_index("dp"), lax.axis_size("dp")
    place = jnp.where(me % 2 == 0, me // 2, count - 1 - me // 2)
    place = (place + offset + count) % count
    return jnp.where(place < count // 2, 2 * place, 2 * (count - 1 - place) + 1)


OFFSETS = [0, -1, 1, -2, 2, -3, 3, 4]


class Gathering:
    def __init__(self, block, earlier=None):
        self.block = held_after(block, earlier)
        self.half = block.shape[0] // 2
        self.whole = None
        self.last = None
        if loop_order(lax.axis_size("dp")) is None:
            self.whole = lax.all_gather(self.block, "dp")
        self.behind, self.ahead = [self.block], [self.block]
        self.step()

    def step(self, token=None):
        if self.whole is not None:
            return
        behind = held_after(self.behind[-1], token)
        ahead = held_after(self.ahead[-1], token)
        if len(self.behind) == 4:
            behind, ahead = behind[: self.half], ahead[self.half :]
        self.behind.append(loop_step(behind, 1))
        self.ahead.append(loop_step(ahead, -1))
        self.last = self.ahead[-1]

    def blocks(self):
        far = jnp.concatenate([self.behind[4], self.ahead[4]], 0)
        near = [self.behind[i] if side == 0 else self.ahead[i] for i in (1, 2, 3) for side in (0, 1)]
        return [self.block] + near + [far]

    def both_parts(self, cuts):
        if self.whole is not None:
            parts = []
            for r, rows, c, columns, groups in cuts:
                part = self.whole[:, r : r + rows, c : c + columns]
                part = part.reshape(part.shape[0], groups, rows // groups, columns)
                parts.append(part.transpose(1, 0, 2, 3))
            return parts, [swap_core(part) for part in parts]
        indices = loop_index(jnp.array(OFFSETS, jnp.int32))
        blocks = self.blocks()
        early = assemble(blocks[:-1], indices[:-1], cuts, len(OFFSETS))
        other = [swap_core(part) for part in early]
        other_block = swap_core(blocks[-1])
        return (
            patch(early, blocks[-1], indices[-1:], cuts),
            patch(other, other_block, indices[-1:], cuts),
        )


class Scattering:
    def __init__(self, chunk, rows):
        self.chunk, self.half = chunk, rows // 2
        self.offset = 4
        self.step()

    def step(self, token=None):
        half = self.half
        if self.offset == 4:
            far = self.chunk(4)
            right, left = far[:half], far[half:]
        else:
            right, left = self.chunk(self.offset), self.chunk(-self.offset)
            if self.offset == 3:
                right = jnp.concatenate([right[:half] + self.right, right[half:]], 0)
                left = jnp.concatenate([left[:half], left[half:] + self.left], 0)
            else:
                right, left = right + self.right, left + self.left
        right = held_after(right.astype(bf16), token)
        left = held_after(left.astype(bf16), token)
        self.right = loop_step(right, 1)
        self.left = self.last = loop_step(left, -1)
        self.offset -= 1

    def total(self):
        return self.chunk(0) + self.right.astype(f32) + self.left.astype(f32)


class Scattered:
    def __init__(self, value):
        self.value, self.last = value, None

    def step(self, token=None):
        pass

    def total(self):
        return self.value


def lay(source, targets, cuts):
    for target, (row, rows, column, columns, groups) in zip(targets, cuts):
        size = rows // groups
        for group in range(groups):
            first = row + group * size
            target[group, 0] = source[first : first + size, column : column + columns]


def slot_spec(cut):
    row, rows, column, columns, groups = cut
    return pl.BlockSpec(
        (groups, 1, rows // groups, columns), lambda i, index: (0, index[i], 0, 0)
    )


def assemble(blocks, indices, cuts, count):
    def body(index_ref, *refs):
        sources, targets = refs[: len(blocks)], refs[len(blocks) :]
        for turn in range(len(blocks)):

            @pl.when(pl.program_id(0) == turn)
            def _():
                lay(sources[turn], targets, cuts)

    whole = [pl.BlockSpec(block.shape, lambda i, index: (0, 0)) for block in blocks]
    shapes = [(groups, count, rows // groups, columns) for _, rows, _, columns, groups in cuts]
    size = sum(block.size for block in blocks) * 4
    return pl.pallas_call(
        body,
        out_shape=[jax.ShapeDtypeStruct(shape, blocks[0].dtype) for shape in shapes],
        grid_spec=pltpu.PrefetchScalarGridSpec(
            num_scalar_prefetch=1,
            grid=(len(blocks),),
            in_specs=whole,
            out_specs=[slot_spec(cut) for cut in cuts],
        ),
        cost_estimate=pl.CostEstimate(flops=0, bytes_accessed=size, transcendentals=0),
        name="assemble",
    )(indices, *blocks)


def patch(parts, block, index, cuts):
    count = len(parts)

    def body(index_ref, *refs):
        lay(refs[count], refs[count + 1 :], cuts)

    return pl.pallas_call(
        body,
        out_shape=[jax.ShapeDtypeStruct(part.shape, part.dtype) for part in parts],
        grid_spec=pltpu.PrefetchScalarGridSpec(
            num_scalar_prefetch=1,
            grid=(1,),
            in_specs=[pl.BlockSpec(memory_space=pl.ANY)] * count
            + [pl.BlockSpec(block.shape, lambda i, index: (0, 0))],
            out_specs=[slot_spec(cut) for cut in cuts],
        ),
        input_output_aliases={i + 1: i for i in range(count)},
        cost_estimate=pl.CostEstimate(flops=0, bytes_accessed=block.size * 4, transcendentals=0),
        name="patch",
    )(index, *parts, block)


def column_cuts(rows, widths, first=0, groups=1):
    return [
        (0, rows, first + sum(widths[:i]), width, groups) for i, width in enumerate(widths)
    ]


def flat_rows(part):
    return part.reshape(-1, part.shape[3])


def scatter_stacks(stacks):
    if loop_order(lax.axis_size("dp")) is None:
        total = sum(jnp.concatenate(stack, 1).astype(f32) for stack in stacks).astype(bf16)
        return Scattered(lax.psum_scatter(total, "dp", scatter_dimension=0).astype(f32))

    def chunk(offset):
        where = loop_index(offset)
        return sum(
            jnp.concatenate(
                [lax.dynamic_index_in_dim(piece, where, 0, keepdims=False) for piece in stack], 0
            ).astype(f32)
            for stack in stacks
        )

    return Scattering(chunk, sum(piece.shape[1] for piece in stacks[0]))


def reroute_plane(pieces, source_of):
    spread = lax.all_to_all(pieces, "dp", split_axis=0, concat_axis=0, tiled=True)
    return lax.all_to_all(spread[source_of], "dp", split_axis=0, concat_axis=0, tiled=True)


def matmul(a, b):
    return jnp.dot(a, b, preferred_element_type=f32)


def contract_last(a, b):
    return lax.dot_general(a, b, (((1,), (1,)), ((), ())), preferred_element_type=f32)


def contract_first(a, b):
    return lax.dot_general(a, b, (((0,), (0,)), ((), ())), preferred_element_type=f32)


def rms_apply(hidden, gain):
    return hidden * lax.rsqrt(jnp.mean(hidden * hidden, axis=-1, keepdims=True) + epsilon) * gain


def norm_back(hidden, gain, upstream):
    scale = lax.rsqrt(jnp.mean(hidden * hidden, axis=-1, keepdims=True) + epsilon)
    weighted = upstream * gain
    dot = jnp.mean(weighted * hidden, axis=-1, keepdims=True)
    grad = scale * weighted - hidden * (scale * scale * scale * dot)
    return grad, jnp.sum(upstream * hidden * scale, axis=0)


PAIR = 2 * DK


def paired(key_columns, value_columns):
    rows, width = key_columns.shape
    both = [part.reshape(rows, width // PAIR, 1, PAIR) for part in (key_columns, value_columns)]
    return jnp.concatenate(both, 2).reshape(rows, 2 * width)


def unpaired(columns):
    rows, width = columns.shape
    both = columns.reshape(rows, width // (2 * PAIR), 2, PAIR)
    return both[:, :, 0].reshape(rows, width // 2), both[:, :, 1].reshape(rows, width // 2)


def lanes_of(head, value):
    lane = lax.broadcasted_iota(jnp.int32, value.shape, 1)
    return jnp.where(lane // DK == head, value, jnp.zeros_like(value))


def dot_last(a, b):
    return lax.dot_general(a, b, (((1,), (1,)), ((), ())), preferred_element_type=f32)


def dot_first(a, b):
    return lax.dot_general(a, b, (((0,), (0,)), ((), ())), preferred_element_type=f32)


def masked_scores(keys, queries, reach):
    scores = dot_last(keys, queries)
    row = lax.broadcasted_iota(jnp.int32, scores.shape, 0)
    return jnp.where(row <= reach, scores, masked_out)


def attend_body(start_ref, query_ref, pair_ref, limit_ref, context_ref, log_ref):
    half = pair_ref.shape[0] // 2
    scaled = query_ref[...] * jnp.asarray(DK ** (-0.5), bf16)
    reach = [limit_ref[...] - start_ref[part] for part in range(2)]
    rows = [pl.ds(part * half, half) for part in range(2)]
    turned = []
    for head in range(2):
        queries = lanes_of(head, scaled)
        scores = [masked_scores(pair_ref[rows[i], :PAIR], queries, reach[i]) for i in range(2)]
        highest = jnp.max(jnp.maximum(scores[0], scores[1]), axis=0, keepdims=True)
        shifted = [jnp.exp(part - highest) for part in scores]
        totals = jnp.sum(shifted[0] + shifted[1], axis=0, keepdims=True)
        context = sum(
            dot_first(pair_ref[rows[i], PAIR:], shifted[i].astype(bf16)) for i in range(2)
        )
        turned.append(context[head * DK : (head + 1) * DK] / totals)
        log_ref[0, head : head + 1] = highest + jnp.log(totals)
    context_ref[...] = jnp.concatenate(turned, 0).T.astype(bf16)


def attend_back_body(
    start_ref, query_ref, pair_ref, limit_ref, log_ref, grad_ref, grad_query_ref, grad_pair_ref
):
    half = pair_ref.shape[0] // 2
    scale = DK ** (-0.5)
    scaled = query_ref[...] * jnp.asarray(scale, bf16)
    reach = [limit_ref[...] - start_ref[part] for part in range(2)]
    rows = [pl.ds(part * half, half) for part in range(2)]
    grad_query = 0.0
    grad_key, grad_value = [0.0, 0.0], [0.0, 0.0]
    for head in range(2):
        queries = lanes_of(head, scaled)
        grad_context = lanes_of(head, grad_ref[...])
        log_total = log_ref[0, head : head + 1]
        weights, grad_weights = [], []
        for i in range(2):
            scores = masked_scores(pair_ref[rows[i], :PAIR], queries, reach[i])
            weights.append(jnp.exp(scores - log_total))
            grad_weights.append(dot_last(pair_ref[rows[i], PAIR:], grad_context))
        inner = jnp.sum(
            weights[0] * grad_weights[0] + weights[1] * grad_weights[1], axis=0, keepdims=True
        )
        for i in range(2):
            grad_scores = (weights[i] * (grad_weights[i] - inner)).astype(bf16)
            grad_value[i] += jnp.dot(
                weights[i].astype(bf16), grad_context, preferred_element_type=f32
            )
            grad_key[i] += jnp.dot(grad_scores, queries, preferred_element_type=f32)
            grad_query += dot_first(lanes_of(head, pair_ref[rows[i], :PAIR]), grad_scores)
    for i in range(2):
        grad_pair_ref[rows[i], :PAIR] = grad_key[i].astype(bf16)
        grad_pair_ref[rows[i], PAIR:] = grad_value[i].astype(bf16)
    grad_query_ref[...] = (grad_query * scale).T.astype(bf16)


def attend_specs(queries, pairs):
    query_spec = pl.BlockSpec((queries.shape[0], PAIR), lambda i, start: (0, i))
    pair_spec = pl.BlockSpec((pairs.shape[0], 2 * PAIR), lambda i, start: (0, i))
    limit_spec = pl.BlockSpec((1, queries.shape[0]), lambda i, start: (0, 0))
    log_spec = pl.BlockSpec((1, 2, queries.shape[0]), lambda i, start: (i, 0, 0))
    return query_spec, pair_spec, limit_spec, log_spec


def attend(queries, pairs, limit, starts):
    query_spec, pair_spec, limit_spec, log_spec = attend_specs(queries, pairs)
    rows, width = queries.shape
    area = rows * pairs.shape[0] * width
    return pl.pallas_call(
        attend_body,
        out_shape=[
            jax.ShapeDtypeStruct((rows, width), bf16),
            jax.ShapeDtypeStruct((width // PAIR, 2, rows), f32),
        ],
        grid_spec=pltpu.PrefetchScalarGridSpec(
            num_scalar_prefetch=1,
            grid=(width // PAIR,),
            in_specs=[query_spec, pair_spec, limit_spec],
            out_specs=[query_spec, log_spec],
        ),
        cost_estimate=pl.CostEstimate(
            flops=area // 64, bytes_accessed=pairs.size // 64, transcendentals=0
        ),
        name="attend",
    )(starts, queries, pairs, limit)


def attend_back(queries, pairs, limit, starts, log_total, grad_context):
    query_spec, pair_spec, limit_spec, log_spec = attend_specs(queries, pairs)
    rows, width = queries.shape
    area = rows * pairs.shape[0] * width
    return pl.pallas_call(
        attend_back_body,
        out_shape=[
            jax.ShapeDtypeStruct((rows, width), bf16),
            jax.ShapeDtypeStruct(pairs.shape, bf16),
        ],
        grid_spec=pltpu.PrefetchScalarGridSpec(
            num_scalar_prefetch=1,
            grid=(width // PAIR,),
            in_specs=[query_spec, pair_spec, limit_spec, log_spec, query_spec],
            out_specs=[query_spec, pair_spec],
        ),
        cost_estimate=pl.CostEstimate(
            flops=area // 64, bytes_accessed=pairs.size // 64, transcendentals=0
        ),
        name="attend_back",
    )(starts, queries, pairs, limit, log_total, grad_context)


def attention_forward(query_in, memory_in, weights, limit, starts, ring=None):
    query_w, pair_w, out_w = weights
    branch, kept = 0.0, []
    for i in range(2):
        queries = matmul(query_in, query_w[i]).astype(bf16)
        pairs = matmul(memory_in, pair_w[i]).astype(bf16)
        if ring is not None:
            queries = held_after(queries, ring.last)
            ring.step()
        context, log_total = attend(queries, pairs, limit, starts)
        branch = branch + contract_last(context, out_w[i])
        kept.append((queries, pairs, context, log_total))
    return branch, kept


def attention_back(kept, weights, limit, starts, grad_rows):
    query_w, pair_w, out_w = weights
    grad_query_in, grad_memory, grads = 0.0, 0.0, []
    for i in range(2):
        queries, pairs, _, log_total = kept[i]
        grad_context = matmul(grad_rows, out_w[i]).astype(bf16)
        grad = attend_back(queries, pairs, limit, starts, log_total, grad_context)
        grad_query_in = grad_query_in + contract_last(grad[0], query_w[i])
        grad_memory = grad_memory + contract_last(grad[1], pair_w[i])
        grads.append(grad)
    return grads, grad_query_in, grad_memory


def attention_weight_grads(query_in, memory_in, kept, grads, grad_rows):
    return [
        jnp.concatenate(
            [
                contract_first(query_in, grads[i][0]).astype(bf16),
                contract_first(memory_in, grads[i][1]).astype(bf16),
                contract_first(grad_rows, kept[i][2]).astype(bf16),
            ],
            1,
        )
        for i in range(2)
    ]


def mlp_forward(normed, gate_up, down):
    width = down[0].shape[1]
    both = [matmul(normed, part) for part in gate_up]
    gate_out = [part[:, :width] for part in both]
    up_out = [part[:, width:] for part in both]
    inner = [
        (jax.nn.gelu(gate, approximate=True) * up).astype(bf16) for gate, up in zip(gate_out, up_out)
    ]
    branch = contract_last(inner[0], down[0]) + contract_last(inner[1], down[1])
    return branch, (both, inner)


def gelu_gate(gate_out, up_out):
    return jax.nn.gelu(gate_out, approximate=True) * up_out


def mlp_back(kept, gate_up, down, grad_rows):
    both, _ = kept
    width = down[0].shape[1]
    grads, total = [], 0.0
    for i in range(2):
        grad_inner = matmul(grad_rows, down[i])
        _, pullback = jax.vjp(gelu_gate, both[i][:, :width], both[i][:, width:])
        grad = jnp.concatenate([part.astype(bf16) for part in pullback(grad_inner)], 1)
        grads.append(grad)
        total = total + contract_last(grad, gate_up[i])
    return grads, total


def mlp_weight_grads(normed, inner, grads, grad_rows):
    return [
        jnp.concatenate(
            [
                contract_first(normed, grads[i]).astype(bf16),
                contract_first(grad_rows, inner[i]).astype(bf16),
            ],
            1,
        )
        for i in range(2)
    ]


def merge_stats(first, second):
    highest = jnp.maximum(first[0], second[0])
    totals = first[1] * jnp.exp(first[0] - highest) + second[1] * jnp.exp(second[0] - highest)
    return jnp.stack([highest, totals, first[2] + second[2]])


def on_device(
    states,
    attn_gain,
    w_query,
    w_key,
    w_value,
    w_out,
    mlp_gain,
    w_gate,
    w_up,
    w_down,
    final_gain,
    cross_gain,
    cross_query,
    cross_key,
    cross_value,
    cross_out,
    embedding,
    source_len,
    target_len,
    target_ids,
    pairing,
):
    slab, me, core = (lax.axis_index(name) for name in ("slab", "dp", "mp"))
    decoding = slab == 1
    count = lax.axis_size("dp")
    numbers = jnp.arange(count, dtype=jnp.int32)
    target_of = jnp.sum(
        jnp.where(pairing[None, :] == numbers[:, None], numbers[None, :], 0), axis=1
    )
    target = target_of[me]
    source_length, target_length = source_len[me], target_len[target]

    gain_rows, cross_rows = attn_gain.shape[1], cross_gain.shape[0]
    width, hidden = w_query.shape[2], w_gate.shape[2]
    half = states.shape[2]
    model = states.shape[3]

    def line_of(value):
        return jnp.pad(value[None], ((0, 0), (0, 4 * width - value.shape[0])))

    extra = jnp.concatenate(
        [
            line_of(jnp.concatenate([attn_gain[0], mlp_gain[0], final_gain[0], cross_gain], 0)),
            line_of((target_ids[0] // 128).astype(bf16)),
            line_of((target_ids[0] % 128).astype(bf16)),
            jnp.zeros((13, 4 * width), bf16),
        ],
        0,
    )

    def attention_block(query_w, key_w, value_w, out_w):
        return jnp.concatenate([query_w, paired(key_w, value_w), out_w.T], 1)

    attention_widths = [width, 2 * width, width]
    cross_block = attention_block(cross_query, cross_key, cross_value, cross_out)
    cross_block = jnp.concatenate([to_decoder(cross_block), cross_block], 0)
    gathering = Gathering(
        jnp.concatenate([attention_block(w_query[0], w_key[0], w_value[0], w_out[0]), extra], 0)
    )
    for _ in range(3):
        gathering.step()
    parts, other_parts = gathering.both_parts(
        column_cuts(gain_rows, attention_widths) + [(gain_rows, 16, 0, 4 * width, 1)]
    )
    self_weights = [
        (flat_rows(part), flat_rows(other)) for part, other in zip(parts[:3], other_parts)
    ]
    extra = parts[3][0]
    gains = extra[:, 0].astype(f32)
    gain_attn, gain_mlp, gain_final = (
        gains[:, i * gain_rows : (i + 1) * gain_rows].reshape(-1) for i in range(3)
    )
    cross_part = gains[:, 3 * gain_rows : 3 * gain_rows + cross_rows].reshape(-1)
    gain_cross = jnp.concatenate([to_decoder(cross_part), cross_part], 0)
    tokens = lax.dynamic_index_in_dim(extra, target, 0, keepdims=False)[:, : 2 * half].astype(f32)
    wanted = (tokens[1] * 128 + tokens[2]).astype(jnp.int32)

    rows = states[0, 0]

    def lend(value):
        cut = value.shape[0] // 2
        lent = jnp.where(decoding, value[cut:], to_encoder(value[:cut]))
        return lent.reshape(count, cut // count, value.shape[1])

    moved = reroute_plane(lend(rows), target_of).reshape(half // 2, model)
    own = jnp.where(decoding, jnp.concatenate([to_decoder(moved), moved], 0), rows)
    other = swap_core(own)

    mlp_gathering = Gathering(
        jnp.concatenate([w_gate[0], w_up[0], w_down[0].T, cross_block], 1), gathering.last
    )

    line = jnp.arange(half, dtype=jnp.int32)
    query_at = core * half + line
    key_at = jnp.concatenate([query_at, (1 - core) * half + line])
    starts = jnp.stack([core * half, (1 - core) * half])
    self_limit = jnp.where(
        decoding, jnp.minimum(query_at, target_length - 1), source_length - 1
    )[None]
    cross_limit = jnp.broadcast_to(source_length - 1, (1, half))

    start = own.astype(f32)
    normed = rms_apply(start, gain_attn).astype(bf16)
    normed_all = jnp.concatenate([normed, rms_apply(other.astype(f32), gain_attn).astype(bf16)], 0)
    branch, self_kept = attention_forward(
        normed,
        normed_all,
        self_weights,
        self_limit,
        starts,
        mlp_gathering,
    )
    after_self = start + branch
    after_self = held_after(after_self, mlp_gathering.last)
    mlp_gathering.step()
    parts, other_parts = mlp_gathering.both_parts(
        column_cuts(gain_rows, [2 * hidden, hidden])
        + column_cuts(2 * cross_rows, attention_widths, 3 * hidden, 2)
    )
    gate_up, down, *cross_weights = [
        (flat_rows(part), flat_rows(other)) for part, other in zip(parts, other_parts)
    ]
    table = lax.all_gather(held_after(embedding, mlp_gathering.last), "dp", axis=0, tiled=True)

    normed_enc = rms_apply(after_self, gain_mlp).astype(bf16)
    branch, enc_kept = mlp_forward(normed_enc, gate_up, down)
    after_enc = after_self + branch
    memory = rms_apply(after_enc, gain_final).astype(bf16)
    memory = to_decoder(memory)
    memory = jnp.concatenate([memory, swap_core(memory)], 0)

    normed_cross = rms_apply(after_self, gain_cross).astype(bf16)
    branch, cross_kept = attention_forward(
        normed_cross,
        memory,
        cross_weights,
        cross_limit,
        starts,
    )
    after_cross = after_self + branch
    normed_dec = rms_apply(after_cross, gain_mlp).astype(bf16)
    branch, dec_kept = mlp_forward(normed_dec, gate_up, down)
    after_mlp = after_cross + branch
    final = rms_apply(after_mlp, gain_final).astype(bf16)

    vocab_rows, cores = embedding.shape[0], lax.axis_size("mp")
    line = jnp.arange(count * vocab_rows, dtype=jnp.int32)
    device = slab * count + line // vocab_rows
    entries = (device * cores + core) * vocab_rows + line % vocab_rows

    final = jnp.where(decoding, final, to_encoder(final))
    final = jnp.concatenate([final, swap_core(final)], 0)
    wanted = jnp.where(core == 0, wanted, jnp.roll(wanted, half))
    counted = key_at < target_length
    width_scale = final.shape[1] ** (-0.5)
    logits = contract_last(final, table) * width_scale
    hits = entries[None, :] == wanted[:, None]
    highest = jnp.max(logits, axis=1)
    totals = jnp.sum(jnp.exp(logits - highest[:, None]), axis=1)
    picked = jnp.sum(jnp.where(hits, logits, 0.0), axis=1)
    stats = jnp.stack([highest, totals, picked])
    flipped = jnp.roll(swap_core(stats), half, axis=1)
    stats = merge_stats(stats, flipped)
    stats = merge_stats(stats, swap_slab(stats))
    log_total = stats[0] + jnp.log(stats[1])
    token_ce = jnp.where(counted, log_total - stats[2], 0.0)
    grad_logits = jnp.where(
        counted[:, None], jnp.exp(logits - log_total[:, None]) - hits.astype(f32), 0.0
    ).astype(bf16)
    grad_final = matmul(grad_logits, table) * width_scale
    grad_final = grad_final[:half] + swap_core(grad_final[half:].astype(bf16)).astype(f32)
    grad_logits = held_after(grad_logits, grad_final)
    grad_final = grad_final + to_decoder(grad_final.astype(bf16)).astype(f32)
    grad_final = jnp.where(decoding, grad_final, 0.0)
    grad_table = (contract_first(grad_logits, final) * width_scale).astype(bf16)
    g_embedding = lax.psum_scatter(grad_table, "dp", scatter_dimension=0, tiled=True)

    stream, grad_gain_final = norm_back(after_mlp, gain_final, grad_final)
    dec_rows = stream.astype(bf16)
    dec_grads, grad_normed = mlp_back(dec_kept, gate_up, down, dec_rows)
    part, grad_gain_mlp = norm_back(after_cross, gain_mlp, grad_normed)
    stream = stream + part
    cross_in = stream.astype(bf16)
    cross_grads, grad_normed, grad_memory = attention_back(
        cross_kept,
        cross_weights,
        cross_limit,
        starts,
        cross_in,
    )
    grad_memory = grad_memory[:half] + swap_core(grad_memory[half:].astype(bf16)).astype(f32)
    cross_in = held_after(cross_in, grad_memory)
    grad_memory = to_encoder(grad_memory.astype(bf16)).astype(f32)
    part, grad_gain_cross = norm_back(after_self, gain_cross, grad_normed)
    stream = stream + part
    cross_sums = attention_weight_grads(normed_cross, memory, cross_kept, cross_grads, cross_in)

    def stacked(part):
        return part.reshape(count, -1, part.shape[1])

    cross_sum = (cross_sums[0].astype(f32) + swap_core(cross_sums[1]).astype(f32)).astype(bf16)
    cut = cross_sum.shape[0] // 2
    cross_sum = jnp.where(decoding, cross_sum[cut:], to_encoder(cross_sum[:cut]))

    enc_stream, gain_part = norm_back(after_enc, gain_final, grad_memory)
    grad_gain_final = grad_gain_final + gain_part
    enc_rows = enc_stream.astype(bf16)
    enc_grads, grad_normed = mlp_back(enc_kept, gate_up, down, enc_rows)
    part, gain_part = norm_back(after_self, gain_mlp, grad_normed)
    grad_gain_mlp = grad_gain_mlp + gain_part
    stream = stream + enc_stream + part
    mlp_sums = lax.cond(
        decoding,
        lambda dec, enc: mlp_weight_grads(*dec),
        lambda dec, enc: mlp_weight_grads(*enc),
        (normed_dec, dec_kept[1], dec_grads, dec_rows),
        (normed_enc, enc_kept[1], enc_grads, held_after(enc_rows, cross_sum)),
    )

    mlp_sum = stacked(mlp_sums[0]).astype(f32) + stacked(swap_core(mlp_sums[1])).astype(f32)
    cross_sum = stacked(cross_sum)
    fold = mlp_sum.shape[1] // cross_sum.shape[1]
    size = cross_sum.shape[2] // fold
    cross_sum = [cross_sum[:, :, i * size : (i + 1) * size] for i in range(fold)]
    packed = jnp.concatenate([mlp_sum.astype(bf16), jnp.concatenate(cross_sum, 1)], 2)
    g_mlp = lax.psum_scatter(packed, "dp", scatter_dimension=0).astype(f32)
    g_cross = jnp.concatenate(jnp.split(g_mlp[:, 3 * hidden :], fold, 0), 1)
    g_mlp = g_mlp[:, : 3 * hidden]

    self_in = held_after(stream.astype(bf16), mlp_sums[0])
    self_grads, grad_normed, grad_keyside = attention_back(
        self_kept,
        self_weights,
        self_limit,
        starts,
        self_in,
    )
    grad_normed = grad_normed + grad_keyside[:half]
    grad_normed = grad_normed + swap_core(grad_keyside[half:].astype(bf16)).astype(f32)
    part, grad_gain_attn = norm_back(start, gain_attn, grad_normed)
    stream = stream + part
    self_sums = attention_weight_grads(normed, normed_all, self_kept, self_grads, self_in)

    in_order = jnp.where(core == 0, token_ce, jnp.roll(token_ce, half)).reshape(count, 1, -1)
    coarse = in_order.astype(bf16)
    fine = (in_order - coarse.astype(f32)).astype(bf16)
    losses = jnp.concatenate([coarse, fine], 2)
    losses = jnp.pad(losses, ((0, 0), (0, 0), (0, model - losses.shape[2])))
    moved = reroute_plane(jnp.concatenate([lend(stream.astype(bf16)), losses], 1), pairing)
    piece = in_order.shape[2]
    losses = moved[:, -1].astype(f32)
    token_loss = (losses[:, :piece] + losses[:, piece : 2 * piece]).reshape(1, -1)
    seq_loss = jnp.sum(token_loss, axis=1) / target_len[me].astype(f32)
    moved = moved[:, :-1].reshape(half // 2, model)
    d_states = jnp.where(
        decoding, jnp.concatenate([to_decoder(moved), moved], 0).astype(f32), stream
    )

    cut = grad_gain_cross.shape[0] // 2
    lent_gains = to_encoder(grad_gain_cross[:cut])
    gain_grads = [grad_gain_attn, grad_gain_mlp, grad_gain_final]
    gain_grads.append(jnp.where(decoding, grad_gain_cross[cut:], lent_gains))
    packed = jnp.concatenate([grad.reshape(count, 1, -1) for grad in gain_grads], 2).astype(bf16)
    packed = jnp.pad(packed, ((0, 0), (0, 15), (0, 4 * width - packed.shape[2])))
    self_scattering = scatter_stacks(
        [[stacked(self_sums[0]), packed], [stacked(swap_core(self_sums[1])), swap_core(packed)]],
    )
    for _ in range(3):
        self_scattering.step()
    g_attn = self_scattering.total()
    gain_own = g_attn[gain_rows : gain_rows + 1]
    g_attn = g_attn[:gain_rows]
    g_key, g_value = unpaired(g_attn[:, width : 3 * width])
    g_cross_key, g_cross_value = unpaired(g_cross[:, width : 3 * width])

    return (
        seq_loss,
        d_states[None, None],
        gain_own[:, :gain_rows],
        g_attn[None, :, :width],
        g_key[None],
        g_value[None],
        g_attn[:, 3 * width :].T[None],
        gain_own[:, gain_rows : 2 * gain_rows],
        g_mlp[None, :, :hidden],
        g_mlp[None, :, hidden : 2 * hidden],
        g_mlp[:, 2 * hidden :].T[None],
        gain_own[:, 2 * gain_rows : 3 * gain_rows],
        gain_own[0, 3 * gain_rows : 3 * gain_rows + cross_rows],
        g_cross[:, :width],
        g_cross_key,
        g_cross_value,
        g_cross[:, 3 * width :].T,
        g_embedding.astype(f32),
        token_loss,
    )


def solution(mesh):
    layer = P("slab", "dp", "mp")
    shared = P(("slab", "dp"), "mp")
    gain = P("slab", "dp")
    turned = P("slab", "mp", "dp")
    tokens = P("slab", "dp", "mp", None)
    weights = (gain, layer, layer, layer, turned, gain, layer, layer, turned, gain)
    crossing = (P(("slab", "dp")), shared, shared, shared, P("mp", ("slab", "dp")))
    table = P(("slab", "dp", "mp"), None)
    return jax.shard_map(
        on_device,
        mesh=mesh,
        in_specs=(tokens,) + weights + crossing + (table, P(), P(), P("dp", None), P()),
        out_specs=(P("dp"), tokens) + weights + crossing + (table, P("dp", None)),
        check_vma=False,
    )
```

```python
import jax
import jax.numpy as jnp
from jax import lax
from jax.experimental import pallas as pl
from jax.experimental.pallas import tpu as pltpu
from jax.sharding import PartitionSpec as P

DK = 64
f32 = jnp.float32
bf16 = jnp.bfloat16
epsilon = 1e-06
masked_out = -1000000000.0


def loop_order(count):
    return [0, 2, 4, 6, 7, 5, 3, 1] if count == 8 else None


def swap_core(value):
    return lax.ppermute(value, "mp", [(0, 1), (1, 0)])


def swap_slab(value):
    return lax.ppermute(value, "slab", [(0, 1), (1, 0)])


def to_encoder(value):
    return lax.ppermute(value, "slab", [(1, 0)])


def to_decoder(value):
    return lax.ppermute(value, "slab", [(0, 1)])


def loop_step(value, step):
    order = loop_order(lax.axis_size("dp"))
    count = len(order)
    pairs = [(order[i], order[(i + step) % count]) for i in range(count)]
    return lax.ppermute(value, "dp", pairs)


def held_after(value, earlier):
    return value if earlier is None else lax.optimization_barrier((value, earlier))[0]


def loop_index(offset):
    me, count = lax.axis_index("dp"), lax.axis_size("dp")
    place = jnp.where(me % 2 == 0, me // 2, count - 1 - me // 2)
    place = (place + offset + count) % count
    return jnp.where(place < count // 2, 2 * place, 2 * (count - 1 - place) + 1)


OFFSETS = [0, -1, 1, -2, 2, -3, 3, 4]


class Gathering:
    def __init__(self, block, earlier=None):
        self.block = held_after(block, earlier)
        self.half = block.shape[0] // 2
        self.whole = None
        self.last = None
        if loop_order(lax.axis_size("dp")) is None:
            self.whole = lax.all_gather(self.block, "dp")
        self.behind, self.ahead = [self.block], [self.block]
        self.step()

    def step(self, token=None):
        if self.whole is not None:
            return
        behind = held_after(self.behind[-1], token)
        ahead = held_after(self.ahead[-1], token)
        if len(self.behind) == 4:
            behind, ahead = behind[: self.half], ahead[self.half :]
        self.behind.append(loop_step(behind, 1))
        self.ahead.append(loop_step(ahead, -1))
        self.last = self.ahead[-1]

    def blocks(self):
        far = jnp.concatenate([self.behind[4], self.ahead[4]], 0)
        near = [self.behind[i] if side == 0 else self.ahead[i] for i in (1, 2, 3) for side in (0, 1)]
        return [self.block] + near + [far]

    def both_parts(self, cuts):
        if self.whole is not None:
            parts = []
            for r, rows, c, columns, groups in cuts:
                part = self.whole[:, r : r + rows, c : c + columns]
                part = part.reshape(part.shape[0], groups, rows // groups, columns)
                parts.append(part.transpose(1, 0, 2, 3))
            return parts, [swap_core(part) for part in parts]
        indices = loop_index(jnp.array(OFFSETS, jnp.int32))
        blocks = self.blocks()
        early = assemble(blocks[:-1], indices[:-1], cuts, len(OFFSETS))
        other = [swap_core(part) for part in early]
        other_block = swap_core(blocks[-1])
        return (
            patch(early, blocks[-1], indices[-1:], cuts),
            patch(other, other_block, indices[-1:], cuts),
        )


class Scattering:
    def __init__(self, chunk, rows):
        self.chunk, self.half = chunk, rows // 2
        self.offset = 4
        self.step()

    def step(self, token=None):
        half = self.half
        if self.offset == 4:
            far = self.chunk(4)
            right, left = far[:half], far[half:]
        else:
            right, left = self.chunk(self.offset), self.chunk(-self.offset)
            if self.offset == 3:
                right = jnp.concatenate([right[:half] + self.right, right[half:]], 0)
                left = jnp.concatenate([left[:half], left[half:] + self.left], 0)
            else:
                right, left = right + self.right, left + self.left
        right = held_after(right.astype(bf16), token)
        left = held_after(left.astype(bf16), token)
        self.right = loop_step(right, 1)
        self.left = self.last = loop_step(left, -1)
        self.offset -= 1

    def total(self):
        return self.chunk(0) + self.right.astype(f32) + self.left.astype(f32)


class Scattered:
    def __init__(self, value):
        self.value, self.last = value, None

    def step(self, token=None):
        pass

    def total(self):
        return self.value


def lay(source, targets, cuts):
    for target, (row, rows, column, columns, groups) in zip(targets, cuts):
        size = rows // groups
        for group in range(groups):
            first = row + group * size
            target[group, 0] = source[first : first + size, column : column + columns]


def slot_spec(cut):
    row, rows, column, columns, groups = cut
    return pl.BlockSpec(
        (groups, 1, rows // groups, columns), lambda i, index: (0, index[i], 0, 0)
    )


def assemble(blocks, indices, cuts, count):
    def body(index_ref, *refs):
        sources, targets = refs[: len(blocks)], refs[len(blocks) :]
        for turn in range(len(blocks)):

            @pl.when(pl.program_id(0) == turn)
            def _():
                lay(sources[turn], targets, cuts)

    whole = [pl.BlockSpec(block.shape, lambda i, index: (0, 0)) for block in blocks]
    shapes = [(groups, count, rows // groups, columns) for _, rows, _, columns, groups in cuts]
    size = sum(block.size for block in blocks) * 4
    return pl.pallas_call(
        body,
        out_shape=[jax.ShapeDtypeStruct(shape, blocks[0].dtype) for shape in shapes],
        grid_spec=pltpu.PrefetchScalarGridSpec(
            num_scalar_prefetch=1,
            grid=(len(blocks),),
            in_specs=whole,
            out_specs=[slot_spec(cut) for cut in cuts],
        ),
        cost_estimate=pl.CostEstimate(flops=0, bytes_accessed=size, transcendentals=0),
        name="assemble",
    )(indices, *blocks)


def patch(parts, block, index, cuts):
    count = len(parts)

    def body(index_ref, *refs):
        lay(refs[count], refs[count + 1 :], cuts)

    return pl.pallas_call(
        body,
        out_shape=[jax.ShapeDtypeStruct(part.shape, part.dtype) for part in parts],
        grid_spec=pltpu.PrefetchScalarGridSpec(
            num_scalar_prefetch=1,
            grid=(1,),
            in_specs=[pl.BlockSpec(memory_space=pl.ANY)] * count
            + [pl.BlockSpec(block.shape, lambda i, index: (0, 0))],
            out_specs=[slot_spec(cut) for cut in cuts],
        ),
        input_output_aliases={i + 1: i for i in range(count)},
        cost_estimate=pl.CostEstimate(flops=0, bytes_accessed=block.size * 4, transcendentals=0),
        name="patch",
    )(index, *parts, block)


def column_cuts(rows, widths, first=0, groups=1):
    return [
        (0, rows, first + sum(widths[:i]), width, groups) for i, width in enumerate(widths)
    ]


def flat_rows(part):
    return part.reshape(-1, part.shape[3])


def scatter_stacks(stacks):
    if loop_order(lax.axis_size("dp")) is None:
        total = sum(jnp.concatenate(stack, 1).astype(f32) for stack in stacks).astype(bf16)
        return Scattered(lax.psum_scatter(total, "dp", scatter_dimension=0).astype(f32))

    def chunk(offset):
        where = loop_index(offset)
        return sum(
            jnp.concatenate(
                [lax.dynamic_index_in_dim(piece, where, 0, keepdims=False) for piece in stack], 0
            ).astype(f32)
            for stack in stacks
        )

    return Scattering(chunk, sum(piece.shape[1] for piece in stacks[0]))


def reroute_plane(pieces, source_of):
    spread = lax.all_to_all(pieces, "dp", split_axis=0, concat_axis=0, tiled=True)
    return lax.all_to_all(spread[source_of], "dp", split_axis=0, concat_axis=0, tiled=True)


def matmul(a, b):
    return jnp.dot(a, b, preferred_element_type=f32)


def contract_last(a, b):
    return lax.dot_general(a, b, (((1,), (1,)), ((), ())), preferred_element_type=f32)


def contract_first(a, b):
    return lax.dot_general(a, b, (((0,), (0,)), ((), ())), preferred_element_type=f32)


def rms_apply(hidden, gain):
    return hidden * lax.rsqrt(jnp.mean(hidden * hidden, axis=-1, keepdims=True) + epsilon) * gain


def norm_back(hidden, gain, upstream):
    scale = lax.rsqrt(jnp.mean(hidden * hidden, axis=-1, keepdims=True) + epsilon)
    weighted = upstream * gain
    dot = jnp.mean(weighted * hidden, axis=-1, keepdims=True)
    grad = scale * weighted - hidden * (scale * scale * scale * dot)
    return grad, jnp.sum(upstream * hidden * scale, axis=0)


PAIR = 2 * DK


def paired(key_columns, value_columns):
    rows, width = key_columns.shape
    both = [part.reshape(rows, width // PAIR, 1, PAIR) for part in (key_columns, value_columns)]
    return jnp.concatenate(both, 2).reshape(rows, 2 * width)


def unpaired(columns):
    rows, width = columns.shape
    both = columns.reshape(rows, width // (2 * PAIR), 2, PAIR)
    return both[:, :, 0].reshape(rows, width // 2), both[:, :, 1].reshape(rows, width // 2)


def lanes_of(head, value):
    lane = lax.broadcasted_iota(jnp.int32, value.shape, 1)
    return jnp.where(lane // DK == head, value, jnp.zeros_like(value))


def dot_last(a, b):
    return lax.dot_general(a, b, (((1,), (1,)), ((), ())), preferred_element_type=f32)


def dot_first(a, b):
    return lax.dot_general(a, b, (((0,), (0,)), ((), ())), preferred_element_type=f32)


def mask_keys(mask_ref, start_ref, limit_ref):
    half = mask_ref.shape[0] // 2

    @pl.when(pl.program_id(0) == 0)
    def _():
        for part in range(2):
            row = lax.broadcasted_iota(jnp.int32, (half, mask_ref.shape[1]), 0)
            reach = limit_ref[...] - start_ref[part]
            mask_ref[part * half : (part + 1) * half] = jnp.where(row <= reach, 0.0, masked_out)


def attend_body(start_ref, query_ref, pair_ref, limit_ref, context_ref, log_ref, mask_ref):
    mask_keys(mask_ref, start_ref, limit_ref)
    scaled = query_ref[...] * jnp.asarray(DK ** (-0.5), bf16)
    turned = []
    for head in range(2):
        scores = dot_last(pair_ref[:, :PAIR], lanes_of(head, scaled)) + mask_ref[...]
        highest = jnp.max(scores, axis=0, keepdims=True)
        shifted = jnp.exp(scores - highest)
        totals = jnp.sum(shifted, axis=0, keepdims=True)
        context = dot_first(pair_ref[:, PAIR:], shifted.astype(bf16))
        turned.append(context[head * DK : (head + 1) * DK] / totals)
        log_ref[0, head : head + 1] = highest + jnp.log(totals)
    context_ref[...] = jnp.concatenate(turned, 0).T.astype(bf16)


def attend_back_body(
    start_ref,
    query_ref,
    pair_ref,
    limit_ref,
    log_ref,
    grad_ref,
    grad_query_ref,
    grad_pair_ref,
    mask_ref,
):
    mask_keys(mask_ref, start_ref, limit_ref)
    scale = DK ** (-0.5)
    scaled = query_ref[...] * jnp.asarray(scale, bf16)
    grad_query, grad_key, grad_value = 0.0, 0.0, 0.0
    for head in range(2):
        queries = lanes_of(head, scaled)
        grad_context = lanes_of(head, grad_ref[...])
        scores = dot_last(pair_ref[:, :PAIR], queries) + mask_ref[...]
        weights = jnp.exp(scores - log_ref[0, head : head + 1])
        grad_weights = dot_last(pair_ref[:, PAIR:], grad_context)
        inner = jnp.sum(weights * grad_weights, axis=0, keepdims=True)
        grad_scores = (weights * (grad_weights - inner)).astype(bf16)
        grad_value += jnp.dot(weights.astype(bf16), grad_context, preferred_element_type=f32)
        grad_key += jnp.dot(grad_scores, queries, preferred_element_type=f32)
        grad_query += dot_first(lanes_of(head, pair_ref[:, :PAIR]), grad_scores)
    grad_pair_ref[:, :PAIR] = grad_key.astype(bf16)
    grad_pair_ref[:, PAIR:] = grad_value.astype(bf16)
    grad_query_ref[...] = (grad_query * scale).T.astype(bf16)


def attend_specs(queries, pairs):
    query_spec = pl.BlockSpec((queries.shape[0], PAIR), lambda i, start: (0, i))
    pair_spec = pl.BlockSpec((pairs.shape[0], 2 * PAIR), lambda i, start: (0, i))
    limit_spec = pl.BlockSpec((1, queries.shape[0]), lambda i, start: (0, 0))
    log_spec = pl.BlockSpec((1, 2, queries.shape[0]), lambda i, start: (i, 0, 0))
    return query_spec, pair_spec, limit_spec, log_spec


def attend(queries, pairs, limit, starts):
    query_spec, pair_spec, limit_spec, log_spec = attend_specs(queries, pairs)
    rows, width = queries.shape
    area = rows * pairs.shape[0] * width
    return pl.pallas_call(
        attend_body,
        out_shape=[
            jax.ShapeDtypeStruct((rows, width), bf16),
            jax.ShapeDtypeStruct((width // PAIR, 2, rows), f32),
        ],
        grid_spec=pltpu.PrefetchScalarGridSpec(
            num_scalar_prefetch=1,
            grid=(width // PAIR,),
            in_specs=[query_spec, pair_spec, limit_spec],
            out_specs=[query_spec, log_spec],
            scratch_shapes=[pltpu.VMEM((pairs.shape[0], rows), f32)],
        ),
        cost_estimate=pl.CostEstimate(
            flops=area // 64, bytes_accessed=pairs.size // 64, transcendentals=0
        ),
        name="attend",
    )(starts, queries, pairs, limit)


def attend_back(queries, pairs, limit, starts, log_total, grad_context):
    query_spec, pair_spec, limit_spec, log_spec = attend_specs(queries, pairs)
    rows, width = queries.shape
    area = rows * pairs.shape[0] * width
    return pl.pallas_call(
        attend_back_body,
        out_shape=[
            jax.ShapeDtypeStruct((rows, width), bf16),
            jax.ShapeDtypeStruct(pairs.shape, bf16),
        ],
        grid_spec=pltpu.PrefetchScalarGridSpec(
            num_scalar_prefetch=1,
            grid=(width // PAIR,),
            in_specs=[query_spec, pair_spec, limit_spec, log_spec, query_spec],
            out_specs=[query_spec, pair_spec],
            scratch_shapes=[pltpu.VMEM((pairs.shape[0], rows), f32)],
        ),
        cost_estimate=pl.CostEstimate(
            flops=area // 64, bytes_accessed=pairs.size // 64, transcendentals=0
        ),
        name="attend_back",
    )(starts, queries, pairs, limit, log_total, grad_context)


def attention_forward(query_in, memory_in, weights, limit, starts, ring=None):
    query_w, pair_w, out_w = weights
    branch, kept = 0.0, []
    for i in range(2):
        queries = matmul(query_in, query_w[i]).astype(bf16)
        pairs = matmul(memory_in, pair_w[i]).astype(bf16)
        if ring is not None:
            queries = held_after(queries, ring.last)
            ring.step()
        context, log_total = attend(queries, pairs, limit, starts)
        branch = branch + contract_last(context, out_w[i])
        kept.append((queries, pairs, context, log_total))
    return branch, kept


def attention_back(kept, weights, limit, starts, grad_rows):
    query_w, pair_w, out_w = weights
    grad_query_in, grad_memory, grads = 0.0, 0.0, []
    for i in range(2):
        queries, pairs, _, log_total = kept[i]
        grad_context = matmul(grad_rows, out_w[i]).astype(bf16)
        grad = attend_back(queries, pairs, limit, starts, log_total, grad_context)
        grad_query_in = grad_query_in + contract_last(grad[0], query_w[i])
        grad_memory = grad_memory + contract_last(grad[1], pair_w[i])
        grads.append(grad)
    return grads, grad_query_in, grad_memory


def row_products(lefts, rights):
    tile = 256
    flat = [right for group in rights for _, right in group]
    widths = [sum(right.shape[1] for _, right in group) for group in rights]
    height = lefts[0].shape[1]

    def body(*refs):
        turned = [ref[...].T for ref in refs[: len(lefts)]]
        sources = iter(refs[len(lefts) : len(lefts) + len(flat)])
        for target, group in zip(refs[len(lefts) + len(flat) :], rights):
            first = 0
            for left, right in group:
                product = jnp.dot(turned[left], next(sources)[...], preferred_element_type=f32)
                target[:, first : first + right.shape[1]] = product.astype(bf16)
                first += right.shape[1]

    return pl.pallas_call(
        body,
        out_shape=[jax.ShapeDtypeStruct((height, width), bf16) for width in widths],
        grid=(height // tile,),
        in_specs=[pl.BlockSpec((left.shape[0], tile), lambda i: (0, i)) for left in lefts]
        + [pl.BlockSpec(right.shape, lambda i: (0, 0)) for right in flat],
        out_specs=[pl.BlockSpec((tile, width), lambda i: (i, 0)) for width in widths],
        cost_estimate=pl.CostEstimate(
            flops=sum(2 * height * right.size for right in flat),
            bytes_accessed=2 * height * sum(widths),
            transcendentals=0,
        ),
        name="row_products",
    )(*lefts, *flat)


def attention_weight_grads(query_in, memory_in, kept, grads, grad_rows):
    return row_products(
        [query_in, memory_in, grad_rows],
        [[(0, grads[i][0]), (1, grads[i][1]), (2, kept[i][2])] for i in range(2)],
    )


def mlp_forward(normed, gate_up, down):
    width = down[0].shape[1]
    both = [matmul(normed, part) for part in gate_up]
    gate_out = [part[:, :width] for part in both]
    up_out = [part[:, width:] for part in both]
    inner = [
        (jax.nn.gelu(gate, approximate=True) * up).astype(bf16) for gate, up in zip(gate_out, up_out)
    ]
    branch = contract_last(inner[0], down[0]) + contract_last(inner[1], down[1])
    return branch, (both, inner)


def gelu_gate(gate_out, up_out):
    return jax.nn.gelu(gate_out, approximate=True) * up_out


def mlp_back(kept, gate_up, down, grad_rows):
    both, _ = kept
    width = down[0].shape[1]
    grads, total = [], 0.0
    for i in range(2):
        grad_inner = matmul(grad_rows, down[i])
        _, pullback = jax.vjp(gelu_gate, both[i][:, :width], both[i][:, width:])
        grad = jnp.concatenate([part.astype(bf16) for part in pullback(grad_inner)], 1)
        grads.append(grad)
        total = total + contract_last(grad, gate_up[i])
    return grads, total


def mlp_weight_grads(normed, inner, grads, grad_rows):
    return row_products(
        [normed, grad_rows], [[(0, grads[i]), (1, inner[i])] for i in range(2)]
    )


def merge_stats(first, second):
    highest = jnp.maximum(first[0], second[0])
    totals = first[1] * jnp.exp(first[0] - highest) + second[1] * jnp.exp(second[0] - highest)
    return jnp.stack([highest, totals, first[2] + second[2]])


def on_device(
    states,
    attn_gain,
    w_query,
    w_key,
    w_value,
    w_out,
    mlp_gain,
    w_gate,
    w_up,
    w_down,
    final_gain,
    cross_gain,
    cross_query,
    cross_key,
    cross_value,
    cross_out,
    embedding,
    source_len,
    target_len,
    target_ids,
    pairing,
):
    slab, me, core = (lax.axis_index(name) for name in ("slab", "dp", "mp"))
    decoding = slab == 1
    count = lax.axis_size("dp")
    numbers = jnp.arange(count, dtype=jnp.int32)
    target_of = jnp.sum(
        jnp.where(pairing[None, :] == numbers[:, None], numbers[None, :], 0), axis=1
    )
    target = target_of[me]
    source_length, target_length = source_len[me], target_len[target]

    gain_rows, cross_rows = attn_gain.shape[1], cross_gain.shape[0]
    width, hidden = w_query.shape[2], w_gate.shape[2]
    half = states.shape[2]
    model = states.shape[3]

    def line_of(value):
        return jnp.pad(value[None], ((0, 0), (0, 4 * width - value.shape[0])))

    extra = jnp.concatenate(
        [
            line_of(jnp.concatenate([attn_gain[0], mlp_gain[0], final_gain[0], cross_gain], 0)),
            line_of((target_ids[0] // 128).astype(bf16)),
            line_of((target_ids[0] % 128).astype(bf16)),
            jnp.zeros((13, 4 * width), bf16),
        ],
        0,
    )

    def attention_block(query_w, key_w, value_w, out_w):
        return jnp.concatenate([query_w, paired(key_w, value_w), out_w.T], 1)

    attention_widths = [width, 2 * width, width]
    cross_block = attention_block(cross_query, cross_key, cross_value, cross_out)
    cross_block = jnp.concatenate([to_decoder(cross_block), cross_block], 0)
    gathering = Gathering(
        jnp.concatenate([attention_block(w_query[0], w_key[0], w_value[0], w_out[0]), extra], 0)
    )
    for _ in range(3):
        gathering.step()
    parts, other_parts = gathering.both_parts(
        column_cuts(gain_rows, attention_widths) + [(gain_rows, 16, 0, 4 * width, 1)]
    )
    self_weights = [
        (flat_rows(part), flat_rows(other)) for part, other in zip(parts[:3], other_parts)
    ]
    extra = parts[3][0]
    gains = extra[:, 0].astype(f32)
    gain_attn, gain_mlp, gain_final = (
        gains[:, i * gain_rows : (i + 1) * gain_rows].reshape(-1) for i in range(3)
    )
    cross_part = gains[:, 3 * gain_rows : 3 * gain_rows + cross_rows].reshape(-1)
    gain_cross = jnp.concatenate([to_decoder(cross_part), cross_part], 0)
    tokens = lax.dynamic_index_in_dim(extra, target, 0, keepdims=False)[:, : 2 * half].astype(f32)
    wanted = (tokens[1] * 128 + tokens[2]).astype(jnp.int32)

    rows = states[0, 0]

    def lend(value):
        cut = value.shape[0] // 2
        lent = jnp.where(decoding, value[cut:], to_encoder(value[:cut]))
        return lent.reshape(count, cut // count, value.shape[1])

    moved = reroute_plane(lend(rows), target_of).reshape(half // 2, model)
    own = jnp.where(decoding, jnp.concatenate([to_decoder(moved), moved], 0), rows)
    other = swap_core(own)

    mlp_gathering = Gathering(
        jnp.concatenate([w_gate[0], w_up[0], w_down[0].T, cross_block], 1), gathering.last
    )

    line = jnp.arange(half, dtype=jnp.int32)
    query_at = core * half + line
    key_at = jnp.concatenate([query_at, (1 - core) * half + line])
    starts = jnp.stack([core * half, (1 - core) * half])
    self_limit = jnp.where(
        decoding, jnp.minimum(query_at, target_length - 1), source_length - 1
    )[None]
    cross_limit = jnp.broadcast_to(source_length - 1, (1, half))

    start = own.astype(f32)
    normed = rms_apply(start, gain_attn).astype(bf16)
    normed_all = jnp.concatenate([normed, rms_apply(other.astype(f32), gain_attn).astype(bf16)], 0)
    branch, self_kept = attention_forward(
        normed,
        normed_all,
        self_weights,
        self_limit,
        starts,
        mlp_gathering,
    )
    after_self = start + branch
    after_self = held_after(after_self, mlp_gathering.last)
    mlp_gathering.step()
    parts, other_parts = mlp_gathering.both_parts(
        column_cuts(gain_rows, [2 * hidden, hidden])
        + column_cuts(2 * cross_rows, attention_widths, 3 * hidden, 2)
    )
    gate_up, down, *cross_weights = [
        (flat_rows(part), flat_rows(other)) for part, other in zip(parts, other_parts)
    ]
    table = lax.all_gather(held_after(embedding, mlp_gathering.last), "dp", axis=0, tiled=True)

    normed_enc = rms_apply(after_self, gain_mlp).astype(bf16)
    branch, enc_kept = mlp_forward(normed_enc, gate_up, down)
    after_enc = after_self + branch
    memory = rms_apply(after_enc, gain_final).astype(bf16)
    memory = to_decoder(memory)
    memory = jnp.concatenate([memory, swap_core(memory)], 0)

    normed_cross = rms_apply(after_self, gain_cross).astype(bf16)
    branch, cross_kept = attention_forward(
        normed_cross,
        memory,
        cross_weights,
        cross_limit,
        starts,
    )
    after_cross = after_self + branch
    normed_dec = rms_apply(after_cross, gain_mlp).astype(bf16)
    branch, dec_kept = mlp_forward(normed_dec, gate_up, down)
    after_mlp = after_cross + branch
    final = rms_apply(after_mlp, gain_final).astype(bf16)

    vocab_rows, cores = embedding.shape[0], lax.axis_size("mp")
    line = jnp.arange(count * vocab_rows, dtype=jnp.int32)
    device = slab * count + line // vocab_rows
    entries = (device * cores + core) * vocab_rows + line % vocab_rows

    final = jnp.where(decoding, final, to_encoder(final))
    final = jnp.concatenate([final, swap_core(final)], 0)
    wanted = jnp.where(core == 0, wanted, jnp.roll(wanted, half))
    counted = key_at < target_length
    width_scale = final.shape[1] ** (-0.5)
    logits = contract_last(final, table) * width_scale
    hits = entries[None, :] == wanted[:, None]
    highest = jnp.max(logits, axis=1)
    totals = jnp.sum(jnp.exp(logits - highest[:, None]), axis=1)
    picked = jnp.sum(jnp.where(hits, logits, 0.0), axis=1)
    stats = jnp.stack([highest, totals, picked])
    flipped = jnp.roll(swap_core(stats), half, axis=1)
    stats = merge_stats(stats, flipped)
    stats = merge_stats(stats, swap_slab(stats))
    log_total = stats[0] + jnp.log(stats[1])
    token_ce = jnp.where(counted, log_total - stats[2], 0.0)
    grad_logits = jnp.where(
        counted[:, None], jnp.exp(logits - log_total[:, None]) - hits.astype(f32), 0.0
    ).astype(bf16)
    grad_final = matmul(grad_logits, table) * width_scale
    grad_final = grad_final[:half] + swap_core(grad_final[half:].astype(bf16)).astype(f32)
    grad_logits = held_after(grad_logits, grad_final)
    grad_final = grad_final + to_decoder(grad_final.astype(bf16)).astype(f32)
    grad_final = jnp.where(decoding, grad_final, 0.0)
    grad_table = (contract_first(grad_logits, final) * width_scale).astype(bf16)
    g_embedding = lax.psum_scatter(grad_table, "dp", scatter_dimension=0, tiled=True)

    stream, grad_gain_final = norm_back(after_mlp, gain_final, grad_final)
    dec_rows = held_after(stream.astype(bf16), grad_table)
    dec_grads, grad_normed = mlp_back(dec_kept, gate_up, down, dec_rows)
    part, grad_gain_mlp = norm_back(after_cross, gain_mlp, grad_normed)
    stream = stream + part
    cross_in = stream.astype(bf16)
    cross_grads, grad_normed, grad_memory = attention_back(
        cross_kept,
        cross_weights,
        cross_limit,
        starts,
        cross_in,
    )
    grad_memory = grad_memory[:half] + swap_core(grad_memory[half:].astype(bf16)).astype(f32)
    cross_in = held_after(cross_in, grad_memory)
    grad_memory = to_encoder(grad_memory.astype(bf16)).astype(f32)
    part, grad_gain_cross = norm_back(after_self, gain_cross, grad_normed)
    stream = stream + part
    cross_sums = attention_weight_grads(normed_cross, memory, cross_kept, cross_grads, cross_in)

    def stacked(part):
        return part.reshape(count, -1, part.shape[1])

    cross_sum = (cross_sums[0].astype(f32) + swap_core(cross_sums[1]).astype(f32)).astype(bf16)

    enc_stream, gain_part = norm_back(after_enc, gain_final, grad_memory)
    grad_gain_final = grad_gain_final + gain_part
    enc_rows = enc_stream.astype(bf16)
    enc_grads, grad_normed = mlp_back(enc_kept, gate_up, down, enc_rows)
    part, gain_part = norm_back(after_self, gain_mlp, grad_normed)
    grad_gain_mlp = grad_gain_mlp + gain_part
    stream = stream + enc_stream + part
    mlp_sums = lax.cond(
        decoding,
        lambda dec, enc: mlp_weight_grads(*dec),
        lambda dec, enc: mlp_weight_grads(*enc),
        (normed_dec, dec_kept[1], dec_grads, dec_rows),
        (normed_enc, enc_kept[1], enc_grads, enc_rows),
    )

    mlp_sum = stacked(mlp_sums[0]).astype(f32) + stacked(swap_core(mlp_sums[1])).astype(f32)
    cut = cross_sum.shape[0] // 2
    halves = jnp.concatenate([stacked(cross_sum[:cut]), stacked(cross_sum[cut:])], 1)
    packed = jnp.concatenate([mlp_sum.astype(bf16), halves], 2)
    summed = lax.psum_scatter(packed, "dp", scatter_dimension=0)
    g_mlp = summed[:, : 3 * hidden].astype(f32)
    g_cross = summed[:, 3 * hidden :]
    g_cross = jnp.where(decoding, g_cross[cross_rows:], to_encoder(g_cross[:cross_rows]))
    g_cross = g_cross.astype(f32)

    self_in = held_after(stream.astype(bf16), packed)
    self_grads, grad_normed, grad_keyside = attention_back(
        self_kept,
        self_weights,
        self_limit,
        starts,
        self_in,
    )
    grad_normed = grad_normed + grad_keyside[:half]
    grad_normed = grad_normed + swap_core(grad_keyside[half:].astype(bf16)).astype(f32)
    part, grad_gain_attn = norm_back(start, gain_attn, grad_normed)
    stream = stream + part
    self_sums = attention_weight_grads(normed, normed_all, self_kept, self_grads, self_in)

    in_order = jnp.where(core == 0, token_ce, jnp.roll(token_ce, half)).reshape(count, 1, -1)
    coarse = in_order.astype(bf16)
    fine = (in_order - coarse.astype(f32)).astype(bf16)
    losses = jnp.concatenate([coarse, fine], 2)
    losses = jnp.pad(losses, ((0, 0), (0, 0), (0, model - losses.shape[2])))
    moved = reroute_plane(jnp.concatenate([lend(stream.astype(bf16)), losses], 1), pairing)
    piece = in_order.shape[2]
    losses = moved[:, -1].astype(f32)
    token_loss = (losses[:, :piece] + losses[:, piece : 2 * piece]).reshape(1, -1)
    seq_loss = jnp.sum(token_loss, axis=1) / target_len[me].astype(f32)
    moved = moved[:, :-1].reshape(half // 2, model)
    d_states = jnp.where(
        decoding, jnp.concatenate([to_decoder(moved), moved], 0).astype(f32), stream
    )

    cut = grad_gain_cross.shape[0] // 2
    lent_gains = to_encoder(grad_gain_cross[:cut])
    gain_grads = [grad_gain_attn, grad_gain_mlp, grad_gain_final]
    gain_grads.append(jnp.where(decoding, grad_gain_cross[cut:], lent_gains))
    lines = jnp.concatenate([grad.reshape(count, 1, -1) for grad in gain_grads], 2).astype(bf16)
    lines = jnp.pad(lines, ((0, 0), (0, 15), (0, 4 * width - lines.shape[2])))
    self_scattering = scatter_stacks(
        [[stacked(self_sums[0]), lines], [stacked(swap_core(self_sums[1])), swap_core(lines)]],
    )
    for _ in range(3):
        self_scattering.step()
    g_attn = self_scattering.total()
    gain_own = g_attn[gain_rows : gain_rows + 1]
    g_attn = g_attn[:gain_rows]
    g_key, g_value = unpaired(g_attn[:, width : 3 * width])
    g_cross_key, g_cross_value = unpaired(g_cross[:, width : 3 * width])

    return (
        seq_loss,
        d_states[None, None],
        gain_own[:, :gain_rows],
        g_attn[None, :, :width],
        g_key[None],
        g_value[None],
        g_attn[:, 3 * width :].T[None],
        gain_own[:, gain_rows : 2 * gain_rows],
        g_mlp[None, :, :hidden],
        g_mlp[None, :, hidden : 2 * hidden],
        g_mlp[:, 2 * hidden :].T[None],
        gain_own[:, 2 * gain_rows : 3 * gain_rows],
        gain_own[0, 3 * gain_rows : 3 * gain_rows + cross_rows],
        g_cross[:, :width],
        g_cross_key,
        g_cross_value,
        g_cross[:, 3 * width :].T,
        g_embedding.astype(f32),
        token_loss,
    )


def solution(mesh):
    layer = P("slab", "dp", "mp")
    shared = P(("slab", "dp"), "mp")
    gain = P("slab", "dp")
    turned = P("slab", "mp", "dp")
    tokens = P("slab", "dp", "mp", None)
    weights = (gain, layer, layer, layer, turned, gain, layer, layer, turned, gain)
    crossing = (P(("slab", "dp")), shared, shared, shared, P("mp", ("slab", "dp")))
    table = P(("slab", "dp", "mp"), None)
    return jax.shard_map(
        on_device,
        mesh=mesh,
        in_specs=(tokens,) + weights + crossing + (table, P(), P(), P("dp", None), P()),
        out_specs=(P("dp"), tokens) + weights + crossing + (table, P("dp", None)),
        check_vma=False,
    )
```

```python
import jax
import jax.numpy as jnp
from jax import lax
from jax.experimental import pallas as pl
from jax.experimental.pallas import tpu as pltpu
from jax.sharding import PartitionSpec as P

DK = 64
f32 = jnp.float32
bf16 = jnp.bfloat16
epsilon = 1e-06
masked_out = -1000000000.0


def loop_order(count):
    return [0, 2, 4, 6, 7, 5, 3, 1] if count == 8 else None


def swap_core(value):
    return lax.ppermute(value, "mp", [(0, 1), (1, 0)])


def swap_slab(value):
    return lax.ppermute(value, "slab", [(0, 1), (1, 0)])


def to_encoder(value):
    return lax.ppermute(value, "slab", [(1, 0)])


def to_decoder(value):
    return lax.ppermute(value, "slab", [(0, 1)])


def loop_step(value, step):
    order = loop_order(lax.axis_size("dp"))
    count = len(order)
    pairs = [(order[i], order[(i + step) % count]) for i in range(count)]
    return lax.ppermute(value, "dp", pairs)


def held_after(value, earlier):
    return value if earlier is None else lax.optimization_barrier((value, earlier))[0]


def loop_index(offset):
    me, count = lax.axis_index("dp"), lax.axis_size("dp")
    place = jnp.where(me % 2 == 0, me // 2, count - 1 - me // 2)
    place = (place + offset + count) % count
    return jnp.where(place < count // 2, 2 * place, 2 * (count - 1 - place) + 1)


OFFSETS = [0, -1, 1, -2, 2, -3, 3, 4]


class Gathering:
    def __init__(self, block, earlier=None):
        self.block = held_after(block, earlier)
        self.half = block.shape[0] // 2
        self.whole = None
        self.last = None
        if loop_order(lax.axis_size("dp")) is None:
            self.whole = lax.all_gather(self.block, "dp")
        self.behind, self.ahead = [self.block], [self.block]
        self.step()

    def step(self, token=None):
        if self.whole is not None:
            return
        behind = held_after(self.behind[-1], token)
        ahead = held_after(self.ahead[-1], token)
        if len(self.behind) == 4:
            behind, ahead = behind[: self.half], ahead[self.half :]
        self.behind.append(loop_step(behind, 1))
        self.ahead.append(loop_step(ahead, -1))
        self.last = self.ahead[-1]

    def blocks(self):
        far = jnp.concatenate([self.behind[4], self.ahead[4]], 0)
        near = [self.behind[i] if side == 0 else self.ahead[i] for i in (1, 2, 3) for side in (0, 1)]
        return [self.block] + near + [far]

    def both_parts(self, cuts):
        if self.whole is not None:
            parts = []
            for r, rows, c, columns, groups in cuts:
                part = self.whole[:, r : r + rows, c : c + columns]
                part = part.reshape(part.shape[0], groups, rows // groups, columns)
                parts.append(part.transpose(1, 0, 2, 3))
            return parts, [swap_core(part) for part in parts]
        indices = loop_index(jnp.array(OFFSETS, jnp.int32))
        blocks = self.blocks()
        early = assemble(blocks[:-1], indices[:-1], cuts, len(OFFSETS))
        other = [swap_core(part) for part in early]
        other_block = swap_core(blocks[-1])
        return (
            patch(early, blocks[-1], indices[-1:], cuts),
            patch(other, other_block, indices[-1:], cuts),
        )


class Scattering:
    def __init__(self, chunk, rows):
        self.chunk, self.half = chunk, rows // 2
        self.offset = 4
        self.step()

    def step(self, token=None):
        half = self.half
        if self.offset == 4:
            far = self.chunk(4)
            right, left = far[:half], far[half:]
        else:
            right, left = self.chunk(self.offset), self.chunk(-self.offset)
            if self.offset == 3:
                right = jnp.concatenate([right[:half] + self.right, right[half:]], 0)
                left = jnp.concatenate([left[:half], left[half:] + self.left], 0)
            else:
                right, left = right + self.right, left + self.left
        right = held_after(right.astype(bf16), token)
        left = held_after(left.astype(bf16), token)
        self.right = loop_step(right, 1)
        self.left = self.last = loop_step(left, -1)
        self.offset -= 1

    def total(self):
        return self.chunk(0) + self.right.astype(f32) + self.left.astype(f32)


class Scattered:
    def __init__(self, value):
        self.value, self.last = value, None

    def step(self, token=None):
        pass

    def total(self):
        return self.value


def lay(source, targets, cuts):
    for target, (row, rows, column, columns, groups) in zip(targets, cuts):
        size = rows // groups
        for group in range(groups):
            first = row + group * size
            target[group, 0] = source[first : first + size, column : column + columns]


def slot_spec(cut):
    row, rows, column, columns, groups = cut
    return pl.BlockSpec(
        (groups, 1, rows // groups, columns), lambda i, index: (0, index[i], 0, 0)
    )


def assemble(blocks, indices, cuts, count):
    def body(index_ref, *refs):
        sources, targets = refs[: len(blocks)], refs[len(blocks) :]
        for turn in range(len(blocks)):

            @pl.when(pl.program_id(0) == turn)
            def _():
                lay(sources[turn], targets, cuts)

    whole = [pl.BlockSpec(block.shape, lambda i, index: (0, 0)) for block in blocks]
    shapes = [(groups, count, rows // groups, columns) for _, rows, _, columns, groups in cuts]
    size = sum(block.size for block in blocks) * 4
    return pl.pallas_call(
        body,
        out_shape=[jax.ShapeDtypeStruct(shape, blocks[0].dtype) for shape in shapes],
        grid_spec=pltpu.PrefetchScalarGridSpec(
            num_scalar_prefetch=1,
            grid=(len(blocks),),
            in_specs=whole,
            out_specs=[slot_spec(cut) for cut in cuts],
        ),
        cost_estimate=pl.CostEstimate(flops=0, bytes_accessed=size, transcendentals=0),
        name="assemble",
    )(indices, *blocks)


def patch(parts, block, index, cuts):
    count = len(parts)

    def body(index_ref, *refs):
        lay(refs[count], refs[count + 1 :], cuts)

    return pl.pallas_call(
        body,
        out_shape=[jax.ShapeDtypeStruct(part.shape, part.dtype) for part in parts],
        grid_spec=pltpu.PrefetchScalarGridSpec(
            num_scalar_prefetch=1,
            grid=(1,),
            in_specs=[pl.BlockSpec(memory_space=pl.ANY)] * count
            + [pl.BlockSpec(block.shape, lambda i, index: (0, 0))],
            out_specs=[slot_spec(cut) for cut in cuts],
        ),
        input_output_aliases={i + 1: i for i in range(count)},
        cost_estimate=pl.CostEstimate(flops=0, bytes_accessed=block.size * 4, transcendentals=0),
        name="patch",
    )(index, *parts, block)


def column_cuts(rows, widths, first=0, groups=1):
    return [
        (0, rows, first + sum(widths[:i]), width, groups) for i, width in enumerate(widths)
    ]


def flat_rows(part):
    return part.reshape(-1, part.shape[3])


def scatter_stacks(stacks):
    if loop_order(lax.axis_size("dp")) is None:
        total = sum(jnp.concatenate(stack, 1).astype(f32) for stack in stacks).astype(bf16)
        return Scattered(lax.psum_scatter(total, "dp", scatter_dimension=0).astype(f32))

    def chunk(offset):
        where = loop_index(offset)
        return sum(
            jnp.concatenate(
                [lax.dynamic_index_in_dim(piece, where, 0, keepdims=False) for piece in stack], 0
            ).astype(f32)
            for stack in stacks
        )

    return Scattering(chunk, sum(piece.shape[1] for piece in stacks[0]))


def reroute_plane(pieces, source_of):
    spread = lax.all_to_all(pieces, "dp", split_axis=0, concat_axis=0, tiled=True)
    return lax.all_to_all(spread[source_of], "dp", split_axis=0, concat_axis=0, tiled=True)


def matmul(a, b):
    return jnp.dot(a, b, preferred_element_type=f32)


def contract_last(a, b):
    return lax.dot_general(a, b, (((1,), (1,)), ((), ())), preferred_element_type=f32)


def contract_first(a, b):
    return lax.dot_general(a, b, (((0,), (0,)), ((), ())), preferred_element_type=f32)


def rms_apply(hidden, gain):
    return hidden * lax.rsqrt(jnp.mean(hidden * hidden, axis=-1, keepdims=True) + epsilon) * gain


def norm_back(hidden, gain, upstream):
    scale = lax.rsqrt(jnp.mean(hidden * hidden, axis=-1, keepdims=True) + epsilon)
    weighted = upstream * gain
    dot = jnp.mean(weighted * hidden, axis=-1, keepdims=True)
    grad = scale * weighted - hidden * (scale * scale * scale * dot)
    return grad, jnp.sum(upstream * hidden * scale, axis=0)


PAIR = 2 * DK


def paired(key_columns, value_columns):
    rows, width = key_columns.shape
    both = [part.reshape(rows, width // PAIR, 1, PAIR) for part in (key_columns, value_columns)]
    return jnp.concatenate(both, 2).reshape(rows, 2 * width)


def unpaired(columns):
    rows, width = columns.shape
    both = columns.reshape(rows, width // (2 * PAIR), 2, PAIR)
    return both[:, :, 0].reshape(rows, width // 2), both[:, :, 1].reshape(rows, width // 2)


def lanes_of(head, value):
    lane = lax.broadcasted_iota(jnp.int32, value.shape, 1)
    return jnp.where(lane // DK == head, value, jnp.zeros_like(value))


def dot_last(a, b):
    return lax.dot_general(a, b, (((1,), (1,)), ((), ())), preferred_element_type=f32)


def dot_first(a, b):
    return lax.dot_general(a, b, (((0,), (0,)), ((), ())), preferred_element_type=f32)


def mask_keys(mask_ref, start_ref, limit_ref):
    half = mask_ref.shape[0] // 2

    @pl.when(pl.program_id(0) == 0)
    def _():
        for part in range(2):
            row = lax.broadcasted_iota(jnp.int32, (half, mask_ref.shape[1]), 0)
            reach = limit_ref[...] - start_ref[part]
            mask_ref[part * half : (part + 1) * half] = jnp.where(row <= reach, 0.0, masked_out)


def attend_body(start_ref, query_ref, pair_ref, limit_ref, context_ref, log_ref, mask_ref):
    mask_keys(mask_ref, start_ref, limit_ref)
    scaled = query_ref[...] * jnp.asarray(DK ** (-0.5), bf16)
    turned = []
    for head in range(2):
        scores = dot_last(pair_ref[:, :PAIR], lanes_of(head, scaled)) + mask_ref[...]
        highest = jnp.max(scores, axis=0, keepdims=True)
        shifted = jnp.exp(scores - highest)
        totals = jnp.sum(shifted, axis=0, keepdims=True)
        context = dot_first(pair_ref[:, PAIR:], shifted.astype(bf16))
        turned.append(context[head * DK : (head + 1) * DK] / totals)
        log_ref[0, head : head + 1] = highest + jnp.log(totals)
    context_ref[...] = jnp.concatenate(turned, 0).T.astype(bf16)


def attend_back_body(
    start_ref,
    query_ref,
    pair_ref,
    limit_ref,
    log_ref,
    grad_ref,
    grad_query_ref,
    grad_pair_ref,
    mask_ref,
):
    mask_keys(mask_ref, start_ref, limit_ref)
    scale = DK ** (-0.5)
    scaled = query_ref[...] * jnp.asarray(scale, bf16)
    grad_query, grad_key, grad_value = 0.0, 0.0, 0.0
    for head in range(2):
        queries = lanes_of(head, scaled)
        grad_context = lanes_of(head, grad_ref[...])
        scores = dot_last(pair_ref[:, :PAIR], queries) + mask_ref[...]
        weights = jnp.exp(scores - log_ref[0, head : head + 1])
        grad_weights = dot_last(pair_ref[:, PAIR:], grad_context)
        inner = jnp.sum(weights * grad_weights, axis=0, keepdims=True)
        grad_scores = (weights * (grad_weights - inner)).astype(bf16)
        grad_value += jnp.dot(weights.astype(bf16), grad_context, preferred_element_type=f32)
        grad_key += jnp.dot(grad_scores, queries, preferred_element_type=f32)
        grad_query += dot_first(lanes_of(head, pair_ref[:, :PAIR]), grad_scores)
    grad_pair_ref[:, :PAIR] = grad_key.astype(bf16)
    grad_pair_ref[:, PAIR:] = grad_value.astype(bf16)
    grad_query_ref[...] = (grad_query * scale).T.astype(bf16)


def attend_specs(queries, pairs):
    query_spec = pl.BlockSpec((queries.shape[0], PAIR), lambda i, start: (0, i))
    pair_spec = pl.BlockSpec((pairs.shape[0], 2 * PAIR), lambda i, start: (0, i))
    limit_spec = pl.BlockSpec((1, queries.shape[0]), lambda i, start: (0, 0))
    log_spec = pl.BlockSpec((1, 2, queries.shape[0]), lambda i, start: (i, 0, 0))
    return query_spec, pair_spec, limit_spec, log_spec


def attend(queries, pairs, limit, starts):
    query_spec, pair_spec, limit_spec, log_spec = attend_specs(queries, pairs)
    rows, width = queries.shape
    area = rows * pairs.shape[0] * width
    return pl.pallas_call(
        attend_body,
        out_shape=[
            jax.ShapeDtypeStruct((rows, width), bf16),
            jax.ShapeDtypeStruct((width // PAIR, 2, rows), f32),
        ],
        grid_spec=pltpu.PrefetchScalarGridSpec(
            num_scalar_prefetch=1,
            grid=(width // PAIR,),
            in_specs=[query_spec, pair_spec, limit_spec],
            out_specs=[query_spec, log_spec],
            scratch_shapes=[pltpu.VMEM((pairs.shape[0], rows), f32)],
        ),
        cost_estimate=pl.CostEstimate(
            flops=area // 64, bytes_accessed=pairs.size // 64, transcendentals=0
        ),
        name="attend",
    )(starts, queries, pairs, limit)


def attend_back(queries, pairs, limit, starts, log_total, grad_context):
    query_spec, pair_spec, limit_spec, log_spec = attend_specs(queries, pairs)
    rows, width = queries.shape
    area = rows * pairs.shape[0] * width
    return pl.pallas_call(
        attend_back_body,
        out_shape=[
            jax.ShapeDtypeStruct((rows, width), bf16),
            jax.ShapeDtypeStruct(pairs.shape, bf16),
        ],
        grid_spec=pltpu.PrefetchScalarGridSpec(
            num_scalar_prefetch=1,
            grid=(width // PAIR,),
            in_specs=[query_spec, pair_spec, limit_spec, log_spec, query_spec],
            out_specs=[query_spec, pair_spec],
            scratch_shapes=[pltpu.VMEM((pairs.shape[0], rows), f32)],
        ),
        cost_estimate=pl.CostEstimate(
            flops=area // 64, bytes_accessed=pairs.size // 64, transcendentals=0
        ),
        name="attend_back",
    )(starts, queries, pairs, limit, log_total, grad_context)


def attention_forward(query_in, memory_in, weights, limit, starts, ring=None):
    query_w, pair_w, out_w = weights
    branch, kept = 0.0, []
    for i in range(2):
        queries = matmul(query_in, query_w[i]).astype(bf16)
        pairs = matmul(memory_in, pair_w[i]).astype(bf16)
        if ring is not None:
            queries = held_after(queries, ring.last)
            ring.step()
        context, log_total = attend(queries, pairs, limit, starts)
        branch = branch + contract_last(context, out_w[i])
        kept.append((queries, pairs, context, log_total))
    return branch, kept


def attention_back(kept, weights, limit, starts, grad_rows):
    query_w, pair_w, out_w = weights
    grad_query_in, grad_memory, grads = 0.0, 0.0, []
    for i in range(2):
        queries, pairs, _, log_total = kept[i]
        grad_context = matmul(grad_rows, out_w[i]).astype(bf16)
        grad = attend_back(queries, pairs, limit, starts, log_total, grad_context)
        grad_query_in = grad_query_in + contract_last(grad[0], query_w[i])
        grad_memory = grad_memory + contract_last(grad[1], pair_w[i])
        grads.append(grad)
    return grads, grad_query_in, grad_memory


def row_products(lefts, rights):
    tile = 256
    flat = [right for group in rights for _, right in group]
    widths = [sum(right.shape[1] for _, right in group) for group in rights]
    height = lefts[0].shape[1]

    def body(*refs):
        turned = [ref[...].T for ref in refs[: len(lefts)]]
        sources = iter(refs[len(lefts) : len(lefts) + len(flat)])
        for target, group in zip(refs[len(lefts) + len(flat) :], rights):
            first = 0
            for left, right in group:
                product = jnp.dot(turned[left], next(sources)[...], preferred_element_type=f32)
                target[:, first : first + right.shape[1]] = product.astype(bf16)
                first += right.shape[1]

    return pl.pallas_call(
        body,
        out_shape=[jax.ShapeDtypeStruct((height, width), bf16) for width in widths],
        grid=(height // tile,),
        in_specs=[pl.BlockSpec((left.shape[0], tile), lambda i: (0, i)) for left in lefts]
        + [pl.BlockSpec(right.shape, lambda i: (0, 0)) for right in flat],
        out_specs=[pl.BlockSpec((tile, width), lambda i: (i, 0)) for width in widths],
        cost_estimate=pl.CostEstimate(
            flops=sum(2 * height * right.size for right in flat),
            bytes_accessed=2 * height * sum(widths),
            transcendentals=0,
        ),
        name="row_products",
    )(*lefts, *flat)


def attention_weight_grads(query_in, memory_in, kept, grads, grad_rows):
    return row_products(
        [query_in, memory_in, grad_rows],
        [[(0, grads[i][0]), (1, grads[i][1]), (2, kept[i][2])] for i in range(2)],
    )


def mlp_forward(normed, gate_up, down):
    width = down[0].shape[1]
    both = [matmul(normed, part) for part in gate_up]
    gate_out = [part[:, :width] for part in both]
    up_out = [part[:, width:] for part in both]
    inner = [
        (jax.nn.gelu(gate, approximate=True) * up).astype(bf16) for gate, up in zip(gate_out, up_out)
    ]
    branch = contract_last(inner[0], down[0]) + contract_last(inner[1], down[1])
    return branch, (both, inner)


def gelu_gate(gate_out, up_out):
    return jax.nn.gelu(gate_out, approximate=True) * up_out


def mlp_back(kept, gate_up, down, grad_rows):
    both, _ = kept
    width = down[0].shape[1]
    grads, total = [], 0.0
    for i in range(2):
        grad_inner = matmul(grad_rows, down[i])
        _, pullback = jax.vjp(gelu_gate, both[i][:, :width], both[i][:, width:])
        grad = jnp.concatenate([part.astype(bf16) for part in pullback(grad_inner)], 1)
        grads.append(grad)
        total = total + contract_last(grad, gate_up[i])
    return grads, total


def mlp_weight_grads(normed, inner, grads, grad_rows):
    return row_products(
        [normed, grad_rows], [[(0, grads[i]), (1, inner[i])] for i in range(2)]
    )


def merge_stats(first, second):
    highest = jnp.maximum(first[0], second[0])
    totals = first[1] * jnp.exp(first[0] - highest) + second[1] * jnp.exp(second[0] - highest)
    return jnp.stack([highest, totals, first[2] + second[2]])


def on_device(
    states,
    attn_gain,
    w_query,
    w_key,
    w_value,
    w_out,
    mlp_gain,
    w_gate,
    w_up,
    w_down,
    final_gain,
    cross_gain,
    cross_query,
    cross_key,
    cross_value,
    cross_out,
    embedding,
    source_len,
    target_len,
    target_ids,
    pairing,
):
    slab, me, core = (lax.axis_index(name) for name in ("slab", "dp", "mp"))
    decoding = slab == 1
    count = lax.axis_size("dp")
    numbers = jnp.arange(count, dtype=jnp.int32)
    target_of = jnp.sum(
        jnp.where(pairing[None, :] == numbers[:, None], numbers[None, :], 0), axis=1
    )
    target = target_of[me]
    source_length, target_length = source_len[me], target_len[target]

    gain_rows, cross_rows = attn_gain.shape[1], cross_gain.shape[0]
    width, hidden = w_query.shape[2], w_gate.shape[2]
    half = states.shape[2]
    model = states.shape[3]

    def line_of(value):
        return jnp.pad(value[None], ((0, 0), (0, 4 * width - value.shape[0])))

    extra = jnp.concatenate(
        [
            line_of(jnp.concatenate([attn_gain[0], mlp_gain[0], final_gain[0], cross_gain], 0)),
            line_of((target_ids[0] // 128).astype(bf16)),
            line_of((target_ids[0] % 128).astype(bf16)),
            jnp.zeros((13, 4 * width), bf16),
        ],
        0,
    )

    def attention_block(query_w, key_w, value_w, out_w):
        return jnp.concatenate([query_w, paired(key_w, value_w), out_w.T], 1)

    attention_widths = [width, 2 * width, width]
    cross_block = attention_block(cross_query, cross_key, cross_value, cross_out)
    cross_block = jnp.concatenate([to_decoder(cross_block), cross_block], 0)
    gathering = Gathering(
        jnp.concatenate([attention_block(w_query[0], w_key[0], w_value[0], w_out[0]), extra], 0)
    )
    for _ in range(3):
        gathering.step()
    parts, other_parts = gathering.both_parts(
        column_cuts(gain_rows, attention_widths) + [(gain_rows, 16, 0, 4 * width, 1)]
    )
    self_weights = [
        (flat_rows(part), flat_rows(other)) for part, other in zip(parts[:3], other_parts)
    ]
    extra = parts[3][0]
    gains = extra[:, 0].astype(f32)
    gain_attn, gain_mlp, gain_final = (
        gains[:, i * gain_rows : (i + 1) * gain_rows].reshape(-1) for i in range(3)
    )
    cross_part = gains[:, 3 * gain_rows : 3 * gain_rows + cross_rows].reshape(-1)
    gain_cross = jnp.concatenate([to_decoder(cross_part), cross_part], 0)
    tokens = lax.dynamic_index_in_dim(extra, target, 0, keepdims=False)[:, : 2 * half].astype(f32)
    wanted = (tokens[1] * 128 + tokens[2]).astype(jnp.int32)

    rows = states[0, 0]

    def lend(value):
        cut = value.shape[0] // 2
        lent = jnp.where(decoding, value[cut:], to_encoder(value[:cut]))
        return lent.reshape(count, cut // count, value.shape[1])

    moved = reroute_plane(lend(rows), target_of).reshape(half // 2, model)
    own = jnp.where(decoding, jnp.concatenate([to_decoder(moved), moved], 0), rows)
    other = swap_core(own)

    mlp_gathering = Gathering(
        jnp.concatenate([w_gate[0], w_up[0], w_down[0].T, cross_block], 1), gathering.last
    )

    line = jnp.arange(half, dtype=jnp.int32)
    query_at = core * half + line
    key_at = jnp.concatenate([query_at, (1 - core) * half + line])
    starts = jnp.stack([core * half, (1 - core) * half])
    self_limit = jnp.where(
        decoding, jnp.minimum(query_at, target_length - 1), source_length - 1
    )[None]
    cross_limit = jnp.broadcast_to(source_length - 1, (1, half))

    start = own.astype(f32)
    normed = rms_apply(start, gain_attn).astype(bf16)
    normed_all = jnp.concatenate([normed, rms_apply(other.astype(f32), gain_attn).astype(bf16)], 0)
    branch, self_kept = attention_forward(
        normed,
        normed_all,
        self_weights,
        self_limit,
        starts,
        mlp_gathering,
    )
    after_self = start + branch
    after_self = held_after(after_self, mlp_gathering.last)
    mlp_gathering.step()
    parts, other_parts = mlp_gathering.both_parts(
        column_cuts(gain_rows, [2 * hidden, hidden])
        + column_cuts(2 * cross_rows, attention_widths, 3 * hidden, 2)
    )
    gate_up, down, *cross_weights = [
        (flat_rows(part), flat_rows(other)) for part, other in zip(parts, other_parts)
    ]
    table = lax.all_gather(held_after(embedding, mlp_gathering.last), "dp", axis=0, tiled=True)

    normed_enc = rms_apply(after_self, gain_mlp).astype(bf16)
    branch, enc_kept = mlp_forward(normed_enc, gate_up, down)
    after_enc = after_self + branch
    memory = rms_apply(after_enc, gain_final).astype(bf16)
    memory = to_decoder(memory)
    memory = jnp.concatenate([memory, swap_core(memory)], 0)

    normed_cross = rms_apply(after_self, gain_cross).astype(bf16)
    branch, cross_kept = attention_forward(
        normed_cross,
        memory,
        cross_weights,
        cross_limit,
        starts,
    )
    after_cross = after_self + branch
    normed_dec = rms_apply(after_cross, gain_mlp).astype(bf16)
    branch, dec_kept = mlp_forward(normed_dec, gate_up, down)
    after_mlp = after_cross + branch
    final = rms_apply(after_mlp, gain_final).astype(bf16)

    vocab_rows, cores = embedding.shape[0], lax.axis_size("mp")
    line = jnp.arange(count * vocab_rows, dtype=jnp.int32)
    device = slab * count + line // vocab_rows
    entries = (device * cores + core) * vocab_rows + line % vocab_rows

    final = jnp.where(decoding, final, to_encoder(final))
    final = jnp.concatenate([final, swap_core(final)], 0)
    wanted = jnp.where(core == 0, wanted, jnp.roll(wanted, half))
    counted = key_at < target_length
    width_scale = final.shape[1] ** (-0.5)
    logits = contract_last(final, table) * width_scale
    hits = entries[None, :] == wanted[:, None]
    highest = jnp.max(logits, axis=1)
    totals = jnp.sum(jnp.exp(logits - highest[:, None]), axis=1)
    picked = jnp.sum(jnp.where(hits, logits, 0.0), axis=1)
    stats = jnp.stack([highest, totals, picked])
    flipped = jnp.roll(swap_core(stats), half, axis=1)
    stats = merge_stats(stats, flipped)
    stats = merge_stats(stats, swap_slab(stats))
    log_total = stats[0] + jnp.log(stats[1])
    token_ce = jnp.where(counted, log_total - stats[2], 0.0)
    grad_logits = jnp.where(
        counted[:, None], jnp.exp(logits - log_total[:, None]) - hits.astype(f32), 0.0
    ).astype(bf16)
    grad_final = matmul(grad_logits, table) * width_scale
    grad_final = grad_final[:half] + swap_core(grad_final[half:].astype(bf16)).astype(f32)
    grad_logits = held_after(grad_logits, grad_final)
    grad_final = grad_final + to_decoder(grad_final.astype(bf16)).astype(f32)
    grad_final = jnp.where(decoding, grad_final, 0.0)
    grad_table = (contract_first(grad_logits, final) * width_scale).astype(bf16)
    g_embedding = lax.psum_scatter(grad_table, "dp", scatter_dimension=0, tiled=True)

    stream, grad_gain_final = norm_back(after_mlp, gain_final, grad_final)
    dec_rows = held_after(stream.astype(bf16), grad_table)
    dec_grads, grad_normed = mlp_back(dec_kept, gate_up, down, dec_rows)
    part, grad_gain_mlp = norm_back(after_cross, gain_mlp, grad_normed)
    stream = stream + part
    cross_in = stream.astype(bf16)
    cross_grads, grad_normed, grad_memory = attention_back(
        cross_kept,
        cross_weights,
        cross_limit,
        starts,
        cross_in,
    )
    grad_memory = grad_memory[:half] + swap_core(grad_memory[half:].astype(bf16)).astype(f32)
    cross_in = held_after(cross_in, grad_memory)
    grad_memory = to_encoder(grad_memory.astype(bf16)).astype(f32)
    part, grad_gain_cross = norm_back(after_self, gain_cross, grad_normed)
    stream = stream + part
    cross_sums = attention_weight_grads(normed_cross, memory, cross_kept, cross_grads, cross_in)

    def stacked(part):
        return part.reshape(count, -1, part.shape[1])

    cross_sum = (cross_sums[0].astype(f32) + swap_core(cross_sums[1]).astype(f32)).astype(bf16)

    enc_stream, gain_part = norm_back(after_enc, gain_final, grad_memory)
    grad_gain_final = grad_gain_final + gain_part
    enc_rows = enc_stream.astype(bf16)
    enc_grads, grad_normed = mlp_back(enc_kept, gate_up, down, enc_rows)
    part, gain_part = norm_back(after_self, gain_mlp, grad_normed)
    grad_gain_mlp = grad_gain_mlp + gain_part
    stream = stream + enc_stream + part
    mlp_sums = lax.cond(
        decoding,
        lambda dec, enc: mlp_weight_grads(*dec),
        lambda dec, enc: mlp_weight_grads(*enc),
        (normed_dec, dec_kept[1], dec_grads, dec_rows),
        (normed_enc, enc_kept[1], enc_grads, enc_rows),
    )

    mlp_sums = lax.optimization_barrier(mlp_sums)
    mlp_sum = stacked(mlp_sums[0]).astype(f32) + stacked(swap_core(mlp_sums[1])).astype(f32)
    cut = cross_sum.shape[0] // 2
    halves = jnp.concatenate([stacked(cross_sum[:cut]), stacked(cross_sum[cut:])], 1)
    packed = jnp.concatenate([mlp_sum.astype(bf16), halves], 2)
    summed = lax.psum_scatter(packed, "dp", scatter_dimension=0)
    g_mlp = summed[:, : 3 * hidden].astype(f32)
    g_cross = summed[:, 3 * hidden :]
    g_cross = jnp.where(decoding, g_cross[cross_rows:], to_encoder(g_cross[:cross_rows]))
    g_cross = g_cross.astype(f32)

    self_in = held_after(stream.astype(bf16), packed)
    self_grads, grad_normed, grad_keyside = attention_back(
        self_kept,
        self_weights,
        self_limit,
        starts,
        self_in,
    )
    grad_normed = grad_normed + grad_keyside[:half]
    grad_normed = grad_normed + swap_core(grad_keyside[half:].astype(bf16)).astype(f32)
    part, grad_gain_attn = norm_back(start, gain_attn, grad_normed)
    stream = stream + part
    self_sums = attention_weight_grads(normed, normed_all, self_kept, self_grads, self_in)

    cut = grad_gain_cross.shape[0] // 2
    lent_gains = to_encoder(grad_gain_cross[:cut])
    gain_grads = [grad_gain_attn, grad_gain_mlp, grad_gain_final]
    gain_grads.append(jnp.where(decoding, grad_gain_cross[cut:], lent_gains))
    lines = jnp.concatenate([grad.reshape(count, 1, -1) for grad in gain_grads], 2).astype(bf16)
    lines = jnp.pad(lines, ((0, 0), (0, 15), (0, 4 * width - lines.shape[2])))
    self_scattering = scatter_stacks(
        [[stacked(self_sums[0]), lines], [stacked(swap_core(self_sums[1])), swap_core(lines)]],
    )
    self_scattering.step()

    in_order = jnp.where(core == 0, token_ce, jnp.roll(token_ce, half)).reshape(count, 1, -1)
    coarse = in_order.astype(bf16)
    fine = (in_order - coarse.astype(f32)).astype(bf16)
    losses = jnp.concatenate([coarse, fine], 2)
    losses = jnp.pad(losses, ((0, 0), (0, 0), (0, model - losses.shape[2])))
    moved = reroute_plane(jnp.concatenate([lend(held_after(stream.astype(bf16), self_scattering.last)), losses], 1), pairing)
    piece = in_order.shape[2]
    losses = moved[:, -1].astype(f32)
    token_loss = (losses[:, :piece] + losses[:, piece : 2 * piece]).reshape(1, -1)
    seq_loss = jnp.sum(token_loss, axis=1) / target_len[me].astype(f32)
    moved = moved[:, :-1].reshape(half // 2, model)
    d_states = jnp.where(
        decoding, jnp.concatenate([to_decoder(moved), moved], 0).astype(f32), stream
    )

    self_scattering.step()
    self_scattering.step()
    g_attn = self_scattering.total()
    gain_own = g_attn[gain_rows : gain_rows + 1]
    g_attn = g_attn[:gain_rows]
    g_key, g_value = unpaired(g_attn[:, width : 3 * width])
    g_cross_key, g_cross_value = unpaired(g_cross[:, width : 3 * width])

    return (
        seq_loss,
        d_states[None, None],
        gain_own[:, :gain_rows],
        g_attn[None, :, :width],
        g_key[None],
        g_value[None],
        g_attn[:, 3 * width :].T[None],
        gain_own[:, gain_rows : 2 * gain_rows],
        g_mlp[None, :, :hidden],
        g_mlp[None, :, hidden : 2 * hidden],
        g_mlp[:, 2 * hidden :].T[None],
        gain_own[:, 2 * gain_rows : 3 * gain_rows],
        gain_own[0, 3 * gain_rows : 3 * gain_rows + cross_rows],
        g_cross[:, :width],
        g_cross_key,
        g_cross_value,
        g_cross[:, 3 * width :].T,
        g_embedding.astype(f32),
        token_loss,
    )


def solution(mesh):
    layer = P("slab", "dp", "mp")
    shared = P(("slab", "dp"), "mp")
    gain = P("slab", "dp")
    turned = P("slab", "mp", "dp")
    tokens = P("slab", "dp", "mp", None)
    weights = (gain, layer, layer, layer, turned, gain, layer, layer, turned, gain)
    crossing = (P(("slab", "dp")), shared, shared, shared, P("mp", ("slab", "dp")))
    table = P(("slab", "dp", "mp"), None)
    return jax.shard_map(
        on_device,
        mesh=mesh,
        in_specs=(tokens,) + weights + crossing + (table, P(), P(), P("dp", None), P()),
        out_specs=(P("dp"), tokens) + weights + crossing + (table, P("dp", None)),
        check_vma=False,
    )
```

```python
import jax
import jax.numpy as jnp
from jax import lax
from jax.experimental import pallas as pl
from jax.experimental.pallas import tpu as pltpu
from jax.sharding import PartitionSpec as P

DK = 64
f32 = jnp.float32
bf16 = jnp.bfloat16
epsilon = 1e-06
masked_out = -1000000000.0


def loop_order(count):
    return [0, 2, 4, 6, 7, 5, 3, 1] if count == 8 else None


def swap_core(value):
    return lax.ppermute(value, "mp", [(0, 1), (1, 0)])


def swap_slab(value):
    return lax.ppermute(value, "slab", [(0, 1), (1, 0)])


def to_encoder(value):
    return lax.ppermute(value, "slab", [(1, 0)])


def to_decoder(value):
    return lax.ppermute(value, "slab", [(0, 1)])


def loop_step(value, step):
    order = loop_order(lax.axis_size("dp"))
    count = len(order)
    pairs = [(order[i], order[(i + step) % count]) for i in range(count)]
    return lax.ppermute(value, "dp", pairs)


def held_after(value, earlier):
    return value if earlier is None else lax.optimization_barrier((value, earlier))[0]


def loop_index(offset):
    me, count = lax.axis_index("dp"), lax.axis_size("dp")
    place = jnp.where(me % 2 == 0, me // 2, count - 1 - me // 2)
    place = (place + offset + count) % count
    return jnp.where(place < count // 2, 2 * place, 2 * (count - 1 - place) + 1)


OFFSETS = [0, -1, 1, -2, 2, -3, 3, 4]


class Gathering:
    def __init__(self, block, earlier=None):
        self.block = held_after(block, earlier)
        self.half = block.shape[0] // 2
        self.whole = None
        self.last = None
        if loop_order(lax.axis_size("dp")) is None:
            self.whole = lax.all_gather(self.block, "dp")
        self.behind, self.ahead = [self.block], [self.block]
        self.step()

    def step(self, token=None):
        if self.whole is not None:
            return
        behind = held_after(self.behind[-1], token)
        ahead = held_after(self.ahead[-1], token)
        if len(self.behind) == 4:
            behind, ahead = behind[: self.half], ahead[self.half :]
        self.behind.append(loop_step(behind, 1))
        self.ahead.append(loop_step(ahead, -1))
        self.last = self.ahead[-1]

    def blocks(self):
        far = jnp.concatenate([self.behind[4], self.ahead[4]], 0)
        near = [self.behind[i] if side == 0 else self.ahead[i] for i in (1, 2, 3) for side in (0, 1)]
        return [self.block] + near + [far]

    def both_parts(self, cuts):
        if self.whole is not None:
            parts = []
            for r, rows, c, columns, groups in cuts:
                part = self.whole[:, r : r + rows, c : c + columns]
                part = part.reshape(part.shape[0], groups, rows // groups, columns)
                parts.append(part.transpose(1, 0, 2, 3))
            return parts, [swap_core(part) for part in parts]
        indices = loop_index(jnp.array(OFFSETS, jnp.int32))
        blocks = self.blocks()
        early = assemble(blocks[:-1], indices[:-1], cuts, len(OFFSETS))
        other = [swap_core(part) for part in early]
        other_block = swap_core(blocks[-1])
        return (
            patch(early, blocks[-1], indices[-1:], cuts),
            patch(other, other_block, indices[-1:], cuts),
        )


class Scattering:
    def __init__(self, chunk, rows):
        self.chunk, self.half = chunk, rows // 2
        self.offset = 4
        self.step()

    def step(self, token=None):
        half = self.half
        if self.offset == 4:
            far = self.chunk(4)
            right, left = far[:half], far[half:]
        else:
            right, left = self.chunk(self.offset), self.chunk(-self.offset)
            if self.offset == 3:
                right = jnp.concatenate([right[:half] + self.right, right[half:]], 0)
                left = jnp.concatenate([left[:half], left[half:] + self.left], 0)
            else:
                right, left = right + self.right, left + self.left
        right = held_after(right.astype(bf16), token)
        left = held_after(left.astype(bf16), token)
        self.right = loop_step(right, 1)
        self.left = self.last = loop_step(left, -1)
        self.offset -= 1

    def total(self):
        return self.chunk(0) + self.right.astype(f32) + self.left.astype(f32)


class Scattered:
    def __init__(self, value):
        self.value, self.last = value, None

    def step(self, token=None):
        pass

    def total(self):
        return self.value


def lay(source, targets, cuts):
    for target, (row, rows, column, columns, groups) in zip(targets, cuts):
        size = rows // groups
        for group in range(groups):
            first = row + group * size
            target[group, 0] = source[first : first + size, column : column + columns]


def slot_spec(cut):
    row, rows, column, columns, groups = cut
    return pl.BlockSpec(
        (groups, 1, rows // groups, columns), lambda i, index: (0, index[i], 0, 0)
    )


def assemble(blocks, indices, cuts, count):
    def body(index_ref, *refs):
        sources, targets = refs[: len(blocks)], refs[len(blocks) :]
        for turn in range(len(blocks)):

            @pl.when(pl.program_id(0) == turn)
            def _():
                lay(sources[turn], targets, cuts)

    whole = [pl.BlockSpec(block.shape, lambda i, index: (0, 0)) for block in blocks]
    shapes = [(groups, count, rows // groups, columns) for _, rows, _, columns, groups in cuts]
    size = sum(block.size for block in blocks) * 4
    return pl.pallas_call(
        body,
        out_shape=[jax.ShapeDtypeStruct(shape, blocks[0].dtype) for shape in shapes],
        grid_spec=pltpu.PrefetchScalarGridSpec(
            num_scalar_prefetch=1,
            grid=(len(blocks),),
            in_specs=whole,
            out_specs=[slot_spec(cut) for cut in cuts],
        ),
        cost_estimate=pl.CostEstimate(flops=0, bytes_accessed=size, transcendentals=0),
        name="assemble",
    )(indices, *blocks)


def patch(parts, block, index, cuts):
    count = len(parts)

    def body(index_ref, *refs):
        lay(refs[count], refs[count + 1 :], cuts)

    return pl.pallas_call(
        body,
        out_shape=[jax.ShapeDtypeStruct(part.shape, part.dtype) for part in parts],
        grid_spec=pltpu.PrefetchScalarGridSpec(
            num_scalar_prefetch=1,
            grid=(1,),
            in_specs=[pl.BlockSpec(memory_space=pl.ANY)] * count
            + [pl.BlockSpec(block.shape, lambda i, index: (0, 0))],
            out_specs=[slot_spec(cut) for cut in cuts],
        ),
        input_output_aliases={i + 1: i for i in range(count)},
        cost_estimate=pl.CostEstimate(flops=0, bytes_accessed=block.size * 4, transcendentals=0),
        name="patch",
    )(index, *parts, block)


def column_cuts(rows, widths, first=0, groups=1):
    return [
        (0, rows, first + sum(widths[:i]), width, groups) for i, width in enumerate(widths)
    ]


def flat_rows(part):
    return part.reshape(-1, part.shape[3])


def scatter_stacks(stacks):
    if loop_order(lax.axis_size("dp")) is None:
        total = sum(jnp.concatenate(stack, 1).astype(f32) for stack in stacks).astype(bf16)
        return Scattered(lax.psum_scatter(total, "dp", scatter_dimension=0).astype(f32))

    def chunk(offset):
        where = loop_index(offset)
        return sum(
            jnp.concatenate(
                [lax.dynamic_index_in_dim(piece, where, 0, keepdims=False) for piece in stack], 0
            ).astype(f32)
            for stack in stacks
        )

    return Scattering(chunk, sum(piece.shape[1] for piece in stacks[0]))


def reroute_plane(pieces, source_of):
    spread = lax.all_to_all(pieces, "dp", split_axis=0, concat_axis=0, tiled=True)
    return lax.all_to_all(spread[source_of], "dp", split_axis=0, concat_axis=0, tiled=True)


def matmul(a, b):
    return jnp.dot(a, b, preferred_element_type=f32)


def contract_last(a, b):
    return lax.dot_general(a, b, (((1,), (1,)), ((), ())), preferred_element_type=f32)


def contract_first(a, b):
    return lax.dot_general(a, b, (((0,), (0,)), ((), ())), preferred_element_type=f32)


def rms_apply(hidden, gain):
    return hidden * lax.rsqrt(jnp.mean(hidden * hidden, axis=-1, keepdims=True) + epsilon) * gain


def norm_back(hidden, gain, upstream):
    scale = lax.rsqrt(jnp.mean(hidden * hidden, axis=-1, keepdims=True) + epsilon)
    weighted = upstream * gain
    dot = jnp.mean(weighted * hidden, axis=-1, keepdims=True)
    grad = scale * weighted - hidden * (scale * scale * scale * dot)
    return grad, jnp.sum(upstream * hidden * scale, axis=0)


PAIR = 2 * DK


def paired(key_columns, value_columns):
    rows, width = key_columns.shape
    both = [part.reshape(rows, width // PAIR, 1, PAIR) for part in (key_columns, value_columns)]
    return jnp.concatenate(both, 2).reshape(rows, 2 * width)


def unpaired(columns):
    rows, width = columns.shape
    both = columns.reshape(rows, width // (2 * PAIR), 2, PAIR)
    return both[:, :, 0].reshape(rows, width // 2), both[:, :, 1].reshape(rows, width // 2)


def lanes_of(head, value):
    lane = lax.broadcasted_iota(jnp.int32, value.shape, 1)
    return jnp.where(lane // DK == head, value, jnp.zeros_like(value))


def dot_last(a, b):
    return lax.dot_general(a, b, (((1,), (1,)), ((), ())), preferred_element_type=f32)


def dot_first(a, b):
    return lax.dot_general(a, b, (((0,), (0,)), ((), ())), preferred_element_type=f32)


def mask_keys(mask_ref, start_ref, limit_ref):
    half = mask_ref.shape[0] // 2

    @pl.when(pl.program_id(0) == 0)
    def _():
        for part in range(2):
            row = lax.broadcasted_iota(jnp.int32, (half, mask_ref.shape[1]), 0)
            reach = limit_ref[...] - start_ref[part]
            mask_ref[part * half : (part + 1) * half] = jnp.where(row <= reach, 0.0, masked_out)


def attend_body(start_ref, query_ref, pair_ref, limit_ref, context_ref, log_ref, mask_ref):
    mask_keys(mask_ref, start_ref, limit_ref)
    scaled = query_ref[...] * jnp.asarray(DK ** (-0.5), bf16)
    turned = []
    for head in range(2):
        scores = dot_last(pair_ref[:, :PAIR], lanes_of(head, scaled)) + mask_ref[...]
        highest = jnp.max(scores, axis=0, keepdims=True)
        shifted = jnp.exp(scores - highest)
        totals = jnp.sum(shifted, axis=0, keepdims=True)
        context = dot_first(pair_ref[:, PAIR:], shifted.astype(bf16))
        turned.append(context[head * DK : (head + 1) * DK] / totals)
        log_ref[0, head : head + 1] = highest + jnp.log(totals)
    context_ref[...] = jnp.concatenate(turned, 0).T.astype(bf16)


def attend_back_body(
    start_ref,
    query_ref,
    pair_ref,
    limit_ref,
    log_ref,
    grad_ref,
    grad_query_ref,
    grad_pair_ref,
    mask_ref,
):
    mask_keys(mask_ref, start_ref, limit_ref)
    scale = DK ** (-0.5)
    scaled = query_ref[...] * jnp.asarray(scale, bf16)
    grad_query, grad_key, grad_value = 0.0, 0.0, 0.0
    for head in range(2):
        queries = lanes_of(head, scaled)
        grad_context = lanes_of(head, grad_ref[...])
        scores = dot_last(pair_ref[:, :PAIR], queries) + mask_ref[...]
        weights = jnp.exp(scores - log_ref[0, head : head + 1])
        grad_weights = dot_last(pair_ref[:, PAIR:], grad_context)
        inner = jnp.sum(weights * grad_weights, axis=0, keepdims=True)
        grad_scores = (weights * (grad_weights - inner)).astype(bf16)
        grad_value += jnp.dot(weights.astype(bf16), grad_context, preferred_element_type=f32)
        grad_key += jnp.dot(grad_scores, queries, preferred_element_type=f32)
        grad_query += dot_first(lanes_of(head, pair_ref[:, :PAIR]), grad_scores)
    grad_pair_ref[:, :PAIR] = grad_key.astype(bf16)
    grad_pair_ref[:, PAIR:] = grad_value.astype(bf16)
    grad_query_ref[...] = (grad_query * scale).T.astype(bf16)


def attend_specs(queries, pairs):
    query_spec = pl.BlockSpec((queries.shape[0], PAIR), lambda i, start: (0, i))
    pair_spec = pl.BlockSpec((pairs.shape[0], 2 * PAIR), lambda i, start: (0, i))
    limit_spec = pl.BlockSpec((1, queries.shape[0]), lambda i, start: (0, 0))
    log_spec = pl.BlockSpec((1, 2, queries.shape[0]), lambda i, start: (i, 0, 0))
    return query_spec, pair_spec, limit_spec, log_spec


def attend(queries, pairs, limit, starts):
    query_spec, pair_spec, limit_spec, log_spec = attend_specs(queries, pairs)
    rows, width = queries.shape
    area = rows * pairs.shape[0] * width
    return pl.pallas_call(
        attend_body,
        out_shape=[
            jax.ShapeDtypeStruct((rows, width), bf16),
            jax.ShapeDtypeStruct((width // PAIR, 2, rows), f32),
        ],
        grid_spec=pltpu.PrefetchScalarGridSpec(
            num_scalar_prefetch=1,
            grid=(width // PAIR,),
            in_specs=[query_spec, pair_spec, limit_spec],
            out_specs=[query_spec, log_spec],
            scratch_shapes=[pltpu.VMEM((pairs.shape[0], rows), f32)],
        ),
        cost_estimate=pl.CostEstimate(
            flops=area // 64, bytes_accessed=pairs.size // 64, transcendentals=0
        ),
        name="attend",
    )(starts, queries, pairs, limit)


def attend_back(queries, pairs, limit, starts, log_total, grad_context):
    query_spec, pair_spec, limit_spec, log_spec = attend_specs(queries, pairs)
    rows, width = queries.shape
    area = rows * pairs.shape[0] * width
    return pl.pallas_call(
        attend_back_body,
        out_shape=[
            jax.ShapeDtypeStruct((rows, width), bf16),
            jax.ShapeDtypeStruct(pairs.shape, bf16),
        ],
        grid_spec=pltpu.PrefetchScalarGridSpec(
            num_scalar_prefetch=1,
            grid=(width // PAIR,),
            in_specs=[query_spec, pair_spec, limit_spec, log_spec, query_spec],
            out_specs=[query_spec, pair_spec],
            scratch_shapes=[pltpu.VMEM((pairs.shape[0], rows), f32)],
        ),
        cost_estimate=pl.CostEstimate(
            flops=area // 64, bytes_accessed=pairs.size // 64, transcendentals=0
        ),
        name="attend_back",
    )(starts, queries, pairs, limit, log_total, grad_context)


def attention_forward(query_in, memory_in, weights, limit, starts, ring=None):
    query_w, pair_w, out_w = weights
    branch, kept = 0.0, []
    for i in range(2):
        queries = matmul(query_in, query_w[i]).astype(bf16)
        pairs = matmul(memory_in, pair_w[i]).astype(bf16)
        if ring is not None:
            queries = held_after(queries, ring.last)
            ring.step()
        context, log_total = attend(queries, pairs, limit, starts)
        branch = branch + contract_last(context, out_w[i])
        kept.append((queries, pairs, context, log_total))
    return branch, kept


def attention_back(kept, weights, limit, starts, grad_rows):
    query_w, pair_w, out_w = weights
    grad_query_in, grad_memory, grads = 0.0, 0.0, []
    for i in range(2):
        queries, pairs, _, log_total = kept[i]
        grad_context = matmul(grad_rows, out_w[i]).astype(bf16)
        grad = attend_back(queries, pairs, limit, starts, log_total, grad_context)
        grad_query_in = grad_query_in + contract_last(grad[0], query_w[i])
        grad_memory = grad_memory + contract_last(grad[1], pair_w[i])
        grads.append(grad)
    return grads, grad_query_in, grad_memory


def row_products(lefts, rights):
    tile = 384
    flat = [right for group in rights for _, right in group]
    widths = [sum(right.shape[1] for _, right in group) for group in rights]
    height = lefts[0].shape[1]

    def body(*refs):
        turned = [ref[...].T for ref in refs[: len(lefts)]]
        sources = iter(refs[len(lefts) : len(lefts) + len(flat)])
        for target, group in zip(refs[len(lefts) + len(flat) :], rights):
            first = 0
            for left, right in group:
                product = jnp.dot(turned[left], next(sources)[...], preferred_element_type=f32)
                target[:, first : first + right.shape[1]] = product.astype(bf16)
                first += right.shape[1]

    return pl.pallas_call(
        body,
        out_shape=[jax.ShapeDtypeStruct((height, width), bf16) for width in widths],
        grid=(height // tile,),
        in_specs=[pl.BlockSpec((left.shape[0], tile), lambda i: (0, i)) for left in lefts]
        + [pl.BlockSpec(right.shape, lambda i: (0, 0)) for right in flat],
        out_specs=[pl.BlockSpec((tile, width), lambda i: (i, 0)) for width in widths],
        cost_estimate=pl.CostEstimate(
            flops=sum(2 * height * right.size for right in flat),
            bytes_accessed=2 * height * sum(widths),
            transcendentals=0,
        ),
        name="row_products",
    )(*lefts, *flat)


def attention_weight_grads(query_in, memory_in, kept, grads, grad_rows):
    return row_products(
        [query_in, memory_in, grad_rows],
        [[(0, grads[i][0]), (1, grads[i][1]), (2, kept[i][2])] for i in range(2)],
    )


def mlp_forward(normed, gate_up, down):
    width = down[0].shape[1]
    both = [matmul(normed, part) for part in gate_up]
    gate_out = [part[:, :width] for part in both]
    up_out = [part[:, width:] for part in both]
    inner = [
        (jax.nn.gelu(gate, approximate=True) * up).astype(bf16) for gate, up in zip(gate_out, up_out)
    ]
    branch = contract_last(inner[0], down[0]) + contract_last(inner[1], down[1])
    return branch, (both, inner)


def gelu_gate(gate_out, up_out):
    return jax.nn.gelu(gate_out, approximate=True) * up_out


def mlp_back(kept, gate_up, down, grad_rows):
    both, _ = kept
    width = down[0].shape[1]
    grads, total = [], 0.0
    for i in range(2):
        grad_inner = matmul(grad_rows, down[i])
        _, pullback = jax.vjp(gelu_gate, both[i][:, :width], both[i][:, width:])
        grad = jnp.concatenate([part.astype(bf16) for part in pullback(grad_inner)], 1)
        grads.append(grad)
        total = total + contract_last(grad, gate_up[i])
    return grads, total


def mlp_weight_grads(normed, inner, grads, grad_rows):
    return row_products(
        [normed, grad_rows], [[(0, grads[i]), (1, inner[i])] for i in range(2)]
    )


def merge_stats(first, second):
    highest = jnp.maximum(first[0], second[0])
    totals = first[1] * jnp.exp(first[0] - highest) + second[1] * jnp.exp(second[0] - highest)
    return jnp.stack([highest, totals, first[2] + second[2]])


def on_device(
    states,
    attn_gain,
    w_query,
    w_key,
    w_value,
    w_out,
    mlp_gain,
    w_gate,
    w_up,
    w_down,
    final_gain,
    cross_gain,
    cross_query,
    cross_key,
    cross_value,
    cross_out,
    embedding,
    source_len,
    target_len,
    target_ids,
    pairing,
):
    slab, me, core = (lax.axis_index(name) for name in ("slab", "dp", "mp"))
    decoding = slab == 1
    count = lax.axis_size("dp")
    numbers = jnp.arange(count, dtype=jnp.int32)
    target_of = jnp.sum(
        jnp.where(pairing[None, :] == numbers[:, None], numbers[None, :], 0), axis=1
    )
    target = target_of[me]
    source_length, target_length = source_len[me], target_len[target]

    gain_rows, cross_rows = attn_gain.shape[1], cross_gain.shape[0]
    width, hidden = w_query.shape[2], w_gate.shape[2]
    half = states.shape[2]
    model = states.shape[3]

    def line_of(value):
        return jnp.pad(value[None], ((0, 0), (0, 4 * width - value.shape[0])))

    extra = jnp.concatenate(
        [
            line_of(jnp.concatenate([attn_gain[0], mlp_gain[0], final_gain[0], cross_gain], 0)),
            line_of((target_ids[0] // 128).astype(bf16)),
            line_of((target_ids[0] % 128).astype(bf16)),
            jnp.zeros((13, 4 * width), bf16),
        ],
        0,
    )

    def attention_block(query_w, key_w, value_w, out_w):
        return jnp.concatenate([query_w, paired(key_w, value_w), out_w.T], 1)

    attention_widths = [width, 2 * width, width]
    cross_block = attention_block(cross_query, cross_key, cross_value, cross_out)
    cross_block = jnp.concatenate([to_decoder(cross_block), cross_block], 0)
    gathering = Gathering(
        jnp.concatenate([attention_block(w_query[0], w_key[0], w_value[0], w_out[0]), extra], 0)
    )
    for _ in range(3):
        gathering.step()
    parts, other_parts = gathering.both_parts(
        column_cuts(gain_rows, attention_widths) + [(gain_rows, 16, 0, 4 * width, 1)]
    )
    self_weights = [
        (flat_rows(part), flat_rows(other)) for part, other in zip(parts[:3], other_parts)
    ]
    extra = parts[3][0]
    gains = extra[:, 0].astype(f32)
    gain_attn, gain_mlp, gain_final = (
        gains[:, i * gain_rows : (i + 1) * gain_rows].reshape(-1) for i in range(3)
    )
    cross_part = gains[:, 3 * gain_rows : 3 * gain_rows + cross_rows].reshape(-1)
    gain_cross = jnp.concatenate([to_decoder(cross_part), cross_part], 0)
    tokens = lax.dynamic_index_in_dim(extra, target, 0, keepdims=False)[:, : 2 * half].astype(f32)
    wanted = (tokens[1] * 128 + tokens[2]).astype(jnp.int32)

    rows = states[0, 0]

    def lend(value):
        cut = value.shape[0] // 2
        lent = jnp.where(decoding, value[cut:], to_encoder(value[:cut]))
        return lent.reshape(count, cut // count, value.shape[1])

    moved = reroute_plane(lend(rows), target_of).reshape(half // 2, model)
    own = jnp.where(decoding, jnp.concatenate([to_decoder(moved), moved], 0), rows)
    other = swap_core(own)

    mlp_gathering = Gathering(
        jnp.concatenate([w_gate[0], w_up[0], w_down[0].T, cross_block], 1), gathering.last
    )

    line = jnp.arange(half, dtype=jnp.int32)
    query_at = core * half + line
    key_at = jnp.concatenate([query_at, (1 - core) * half + line])
    starts = jnp.stack([core * half, (1 - core) * half])
    self_limit = jnp.where(
        decoding, jnp.minimum(query_at, target_length - 1), source_length - 1
    )[None]
    cross_limit = jnp.broadcast_to(source_length - 1, (1, half))

    start = own.astype(f32)
    normed = rms_apply(start, gain_attn).astype(bf16)
    normed_all = jnp.concatenate([normed, rms_apply(other.astype(f32), gain_attn).astype(bf16)], 0)
    branch, self_kept = attention_forward(
        normed,
        normed_all,
        self_weights,
        self_limit,
        starts,
        mlp_gathering,
    )
    after_self = start + branch
    after_self = held_after(after_self, mlp_gathering.last)
    mlp_gathering.step()
    parts, other_parts = mlp_gathering.both_parts(
        column_cuts(gain_rows, [2 * hidden, hidden])
        + column_cuts(2 * cross_rows, attention_widths, 3 * hidden, 2)
    )
    gate_up, down, *cross_weights = [
        (flat_rows(part), flat_rows(other)) for part, other in zip(parts, other_parts)
    ]
    table = lax.all_gather(held_after(embedding, mlp_gathering.last), "dp", axis=0, tiled=True)

    normed_enc = rms_apply(after_self, gain_mlp).astype(bf16)
    branch, enc_kept = mlp_forward(normed_enc, gate_up, down)
    after_enc = after_self + branch
    memory = rms_apply(after_enc, gain_final).astype(bf16)
    memory = to_decoder(memory)
    memory = jnp.concatenate([memory, swap_core(memory)], 0)

    normed_cross = rms_apply(after_self, gain_cross).astype(bf16)
    branch, cross_kept = attention_forward(
        normed_cross,
        memory,
        cross_weights,
        cross_limit,
        starts,
    )
    after_cross = after_self + branch
    normed_dec = rms_apply(after_cross, gain_mlp).astype(bf16)
    branch, dec_kept = mlp_forward(normed_dec, gate_up, down)
    after_mlp = after_cross + branch
    final = rms_apply(after_mlp, gain_final).astype(bf16)

    vocab_rows, cores = embedding.shape[0], lax.axis_size("mp")
    line = jnp.arange(count * vocab_rows, dtype=jnp.int32)
    device = slab * count + line // vocab_rows
    entries = (device * cores + core) * vocab_rows + line % vocab_rows

    final = jnp.where(decoding, final, to_encoder(final))
    final = jnp.concatenate([final, swap_core(final)], 0)
    wanted = jnp.where(core == 0, wanted, jnp.roll(wanted, half))
    counted = key_at < target_length
    width_scale = final.shape[1] ** (-0.5)
    logits = contract_last(final, table) * width_scale
    hits = entries[None, :] == wanted[:, None]
    highest = jnp.max(logits, axis=1)
    totals = jnp.sum(jnp.exp(logits - highest[:, None]), axis=1)
    picked = jnp.sum(jnp.where(hits, logits, 0.0), axis=1)
    stats = jnp.stack([highest, totals, picked])
    flipped = jnp.roll(swap_core(stats), half, axis=1)
    stats = merge_stats(stats, flipped)
    stats = merge_stats(stats, swap_slab(stats))
    log_total = stats[0] + jnp.log(stats[1])
    token_ce = jnp.where(counted, log_total - stats[2], 0.0)
    grad_logits = jnp.where(
        counted[:, None], jnp.exp(logits - log_total[:, None]) - hits.astype(f32), 0.0
    ).astype(bf16)
    grad_final = matmul(grad_logits, table) * width_scale
    grad_final = grad_final[:half] + swap_core(grad_final[half:].astype(bf16)).astype(f32)
    grad_logits = held_after(grad_logits, grad_final)
    grad_final = grad_final + to_decoder(grad_final.astype(bf16)).astype(f32)
    grad_final = jnp.where(decoding, grad_final, 0.0)
    grad_table = (contract_first(grad_logits, final) * width_scale).astype(bf16)
    g_embedding = lax.psum_scatter(grad_table, "dp", scatter_dimension=0, tiled=True)

    stream, grad_gain_final = norm_back(after_mlp, gain_final, grad_final)
    dec_rows = held_after(stream.astype(bf16), grad_table)
    dec_grads, grad_normed = mlp_back(dec_kept, gate_up, down, dec_rows)
    part, grad_gain_mlp = norm_back(after_cross, gain_mlp, grad_normed)
    stream = stream + part
    cross_in = stream.astype(bf16)
    cross_grads, grad_normed, grad_memory = attention_back(
        cross_kept,
        cross_weights,
        cross_limit,
        starts,
        cross_in,
    )
    grad_memory = grad_memory[:half] + swap_core(grad_memory[half:].astype(bf16)).astype(f32)
    cross_in = held_after(cross_in, grad_memory)
    grad_memory = to_encoder(grad_memory.astype(bf16)).astype(f32)
    part, grad_gain_cross = norm_back(after_self, gain_cross, grad_normed)
    stream = stream + part
    cross_sums = attention_weight_grads(normed_cross, memory, cross_kept, cross_grads, cross_in)

    def stacked(part):
        return part.reshape(count, -1, part.shape[1])

    cross_sum = (cross_sums[0].astype(f32) + swap_core(cross_sums[1]).astype(f32)).astype(bf16)

    enc_stream, gain_part = norm_back(after_enc, gain_final, grad_memory)
    grad_gain_final = grad_gain_final + gain_part
    enc_rows = enc_stream.astype(bf16)
    enc_grads, grad_normed = mlp_back(enc_kept, gate_up, down, enc_rows)
    part, gain_part = norm_back(after_self, gain_mlp, grad_normed)
    grad_gain_mlp = grad_gain_mlp + gain_part
    stream = stream + enc_stream + part
    mlp_sums = lax.cond(
        decoding,
        lambda dec, enc: mlp_weight_grads(*dec),
        lambda dec, enc: mlp_weight_grads(*enc),
        (normed_dec, dec_kept[1], dec_grads, dec_rows),
        (normed_enc, enc_kept[1], enc_grads, enc_rows),
    )

    mlp_sums = lax.optimization_barrier(mlp_sums)
    mlp_sum = stacked(mlp_sums[0]).astype(f32) + stacked(swap_core(mlp_sums[1])).astype(f32)
    cut = cross_sum.shape[0] // 2
    halves = jnp.concatenate([stacked(cross_sum[:cut]), stacked(cross_sum[cut:])], 1)
    packed = jnp.concatenate([mlp_sum.astype(bf16), halves], 2)
    summed = lax.psum_scatter(packed, "dp", scatter_dimension=0)
    g_mlp = summed[:, : 3 * hidden].astype(f32)
    g_cross = summed[:, 3 * hidden :]
    g_cross = jnp.where(decoding, g_cross[cross_rows:], to_encoder(g_cross[:cross_rows]))
    g_cross = g_cross.astype(f32)

    self_in = held_after(stream.astype(bf16), packed)
    self_grads, grad_normed, grad_keyside = attention_back(
        self_kept,
        self_weights,
        self_limit,
        starts,
        self_in,
    )
    grad_normed = grad_normed + grad_keyside[:half]
    grad_normed = grad_normed + swap_core(grad_keyside[half:].astype(bf16)).astype(f32)
    part, grad_gain_attn = norm_back(start, gain_attn, grad_normed)
    stream = stream + part
    self_sums = attention_weight_grads(normed, normed_all, self_kept, self_grads, self_in)

    cut = grad_gain_cross.shape[0] // 2
    lent_gains = to_encoder(grad_gain_cross[:cut])
    gain_grads = [grad_gain_attn, grad_gain_mlp, grad_gain_final]
    gain_grads.append(jnp.where(decoding, grad_gain_cross[cut:], lent_gains))
    lines = jnp.concatenate([grad.reshape(count, 1, -1) for grad in gain_grads], 2).astype(bf16)
    lines = jnp.pad(lines, ((0, 0), (0, 15), (0, 4 * width - lines.shape[2])))
    self_scattering = scatter_stacks(
        [[stacked(self_sums[0]), lines], [stacked(swap_core(self_sums[1])), swap_core(lines)]],
    )
    self_scattering.step()

    in_order = jnp.where(core == 0, token_ce, jnp.roll(token_ce, half)).reshape(count, 1, -1)
    coarse = in_order.astype(bf16)
    fine = (in_order - coarse.astype(f32)).astype(bf16)
    losses = jnp.concatenate([coarse, fine], 2)
    losses = jnp.pad(losses, ((0, 0), (0, 0), (0, model - losses.shape[2])))
    moved = reroute_plane(jnp.concatenate([lend(held_after(stream.astype(bf16), self_scattering.last)), losses], 1), pairing)
    piece = in_order.shape[2]
    losses = moved[:, -1].astype(f32)
    token_loss = (losses[:, :piece] + losses[:, piece : 2 * piece]).reshape(1, -1)
    seq_loss = jnp.sum(token_loss, axis=1) / target_len[me].astype(f32)
    moved = moved[:, :-1].reshape(half // 2, model)
    d_states = jnp.where(
        decoding, jnp.concatenate([to_decoder(moved), moved], 0).astype(f32), stream
    )

    self_scattering.step()
    self_scattering.step()
    g_attn = self_scattering.total()
    gain_own = g_attn[gain_rows : gain_rows + 1]
    g_attn = g_attn[:gain_rows]
    g_key, g_value = unpaired(g_attn[:, width : 3 * width])
    g_cross_key, g_cross_value = unpaired(g_cross[:, width : 3 * width])

    return (
        seq_loss,
        d_states[None, None],
        gain_own[:, :gain_rows],
        g_attn[None, :, :width],
        g_key[None],
        g_value[None],
        g_attn[:, 3 * width :].T[None],
        gain_own[:, gain_rows : 2 * gain_rows],
        g_mlp[None, :, :hidden],
        g_mlp[None, :, hidden : 2 * hidden],
        g_mlp[:, 2 * hidden :].T[None],
        gain_own[:, 2 * gain_rows : 3 * gain_rows],
        gain_own[0, 3 * gain_rows : 3 * gain_rows + cross_rows],
        g_cross[:, :width],
        g_cross_key,
        g_cross_value,
        g_cross[:, 3 * width :].T,
        g_embedding.astype(f32),
        token_loss,
    )


def solution(mesh):
    layer = P("slab", "dp", "mp")
    shared = P(("slab", "dp"), "mp")
    gain = P("slab", "dp")
    turned = P("slab", "mp", "dp")
    tokens = P("slab", "dp", "mp", None)
    weights = (gain, layer, layer, layer, turned, gain, layer, layer, turned, gain)
    crossing = (P(("slab", "dp")), shared, shared, shared, P("mp", ("slab", "dp")))
    table = P(("slab", "dp", "mp"), None)
    return jax.shard_map(
        on_device,
        mesh=mesh,
        in_specs=(tokens,) + weights + crossing + (table, P(), P(), P("dp", None), P()),
        out_specs=(P("dp"), tokens) + weights + crossing + (table, P("dp", None)),
        check_vma=False,
    )
```
